32 devices in a mesh: dp: 4 (over y, core), seq: 2 (over x), mp: 4 (over z).
Axes of the slice: x: 2, y: 2, z: 4, core: 2. Of those that a mesh axis runs over, the one named last changes fastest.
Arguments:
- acts: bfloat16 [4, 1024, 2, 768], P('dp', 'mp', 'seq'), may hold values from -6 to 6
- cotangent: bfloat16 [4, 1024, 2, 768], P('dp', 'mp', 'seq'), may hold values from -8 to 8
- col_mask: int32 [4, 1024], P('dp'), may hold values from 0 to 1, as said below
- ln_row_gain: float32 [1, 768], replicated, may hold values from 0.5 to 1.5
- ln_row_bias: float32 [1, 768], replicated, may hold values from -1.25 to 1.25
- row_wq: bfloat16 [1, 768, 768], P(None, None, 'mp'), may hold values from -0.21875 to 0.21875
- row_wk: bfloat16 [1, 768, 768], P(None, None, 'mp'), may hold values from -0.21875 to 0.21875
- row_wv: bfloat16 [1, 768, 768], P(None, None, 'mp'), may hold values from -0.21875 to 0.21875
- row_bq: float32 [1, 768], P(None, 'mp'), may hold values from -1.25 to 1.25
- row_bv: float32 [1, 768], P(None, 'mp'), may hold values from -1.25 to 1.25
- row_wo: bfloat16 [1, 768, 768], P(None, 'mp'), may hold values from -0.875 to 0.875
- row_bo: float32 [1, 768], replicated, may hold values from -1.25 to 1.25
- ln_col_gain: float32 [1, 768], replicated, may hold values from 0.5 to 1.5
- ln_col_bias: float32 [1, 768], replicated, may hold values from -1.25 to 1.25
- col_wq: bfloat16 [1, 768, 768], P(None, None, 'mp'), may hold values from -0.21875 to 0.21875
- col_wk: bfloat16 [1, 768, 768], P(None, None, 'mp'), may hold values from -0.21875 to 0.21875
- col_wv: bfloat16 [1, 768, 768], P(None, None, 'mp'), may hold values from -0.21875 to 0.21875
- col_bq: float32 [1, 768], P(None, 'mp'), may hold values from -1.25 to 1.25
- col_bv: float32 [1, 768], P(None, 'mp'), may hold values from -1.25 to 1.25
- col_wo: bfloat16 [1, 768, 768], P(None, 'mp'), may hold values from -0.4375 to 0.4375
- col_bo: float32 [1, 768], replicated, may hold values from -1.25 to 1.25
- ln_ffn_gain: float32 [1, 768], replicated, may hold values from 0.5 to 1.5
- ln_ffn_bias: float32 [1, 768], replicated, may hold values from -1.25 to 1.25
- ffn_w1: bfloat16 [1, 768, 3072], P(None, None, 'mp'), may hold values from -0.21875 to 0.21875
- ffn_b1: float32 [1, 3072], P(None, 'mp'), may hold values from -1.25 to 1.25
- ffn_w2: bfloat16 [1, 3072, 768], P(None, 'mp'), may hold values from -0.15625 to 0.15625
- ffn_b2: float32 [1, 768], replicated, may hold values from -1.25 to 1.25
Outputs:
- out: float32 [4, 1024, 2, 768], P('dp', 'mp', 'seq')
- grad_acts: float32 [4, 1024, 2, 768], P('dp', 'mp', 'seq')
- grad_ln_row_gain: float32 [1, 768], P(None, ('dp', 'seq', 'mp'))
- grad_ln_row_bias: float32 [1, 768], P(None, ('dp', 'seq', 'mp'))
- grad_row_wq: float32 [1, 768, 768], P(None, ('dp', 'seq'), 'mp')
- grad_row_wk: float32 [1, 768, 768], P(None, ('dp', 'seq'), 'mp')
- grad_row_wv: float32 [1, 768, 768], P(None, ('dp', 'seq'), 'mp')
- grad_row_bq: float32 [1, 768], P(None, 'mp')
- grad_row_bv: float32 [1, 768], P(None, 'mp')
- grad_row_wo: float32 [1, 768, 768], P(None, 'mp', ('dp', 'seq'))
- grad_row_bo: float32 [1, 768], P(None, ('dp', 'seq', 'mp'))
- grad_ln_col_gain: float32 [1, 768], P(None, ('dp', 'seq', 'mp'))
- grad_ln_col_bias: float32 [1, 768], P(None, ('dp', 'seq', 'mp'))
- grad_col_wq: float32 [1, 768, 768], P(None, ('dp', 'seq'), 'mp')
- grad_col_wk: float32 [1, 768, 768], P(None, ('dp', 'seq'), 'mp')
- grad_col_wv: float32 [1, 768, 768], P(None, ('dp', 'seq'), 'mp')
- grad_col_bq: float32 [1, 768], P(None, 'mp')
- grad_col_bv: float32 [1, 768], P(None, 'mp')
- grad_col_wo: float32 [1, 768, 768], P(None, 'mp', ('dp', 'seq'))
- grad_col_bo: float32 [1, 768], P(None, ('dp', 'seq', 'mp'))
- grad_ln_ffn_gain: float32 [1, 768], P(None, ('dp', 'seq', 'mp'))
- grad_ln_ffn_bias: float32 [1, 768], P(None, ('dp', 'seq', 'mp'))
- grad_ffn_w1: float32 [1, 768, 3072], P(None, ('dp', 'seq'), 'mp')
- grad_ffn_b1: float32 [1, 3072], P(None, 'mp')
- grad_ffn_w2: float32 [1, 3072, 768], P(None, 'mp', ('dp', 'seq'))
- grad_ffn_b2: float32 [1, 768], P(None, ('dp', 'seq', 'mp'))
The draws below stay inside these ranges and needn't reach their ends.
Inputs may be any that keep to these rules, and one draw needn't show every extreme that they name: `col_mask`: in each alignment the valid columns are a leading run of 64 to 1024 columns; some alignment has all 1024 columns valid.
All inputs are finite; a program needn't handle non-finite values.
Results may differ from the reference program's by a relative error of at most 0.035.
Values may be sent and summed in bfloat16 or wider, within the bound.
No kernel may reach another device: no remote copies, remote signals or barrier semaphores. Data moves between devices by JAX's collectives and lax.ppermute only.
A program may use at most 192 MiB of HBM per device.

```python
import math
import jax
import jax.numpy as jnp
from jax import lax

D = 768
HD = 64
FF = 3072
C = 1024
MIN_LEN = 64
LAYERS = 1
ROWS = 2
ALIGN = 4


def draw_col_mask(key, part):
    length_key = jax.random.fold_in(key, 11)
    full_key = jax.random.fold_in(key, 23)
    lengths = jax.random.randint(length_key, (ALIGN,), MIN_LEN, C + 1)
    chosen = jax.random.randint(full_key, (), 0, ALIGN)
    lengths = jnp.where(jnp.arange(ALIGN) == chosen, C, lengths)
    positions = jnp.arange(C)
    return (positions[None, :] < lengths[:, None]).astype(jnp.int32)


def strengthened(values, own_key, source, target, shards_of, factor):
    owner, partner = [(jnp.arange(values.shape[axis_at]) // (values.shape[axis_at] // shards_of)).reshape([-1 if axis == axis_at else 1 for axis in range(values.ndim)]) for axis_at in (source, target)]
    chosen = jax.random.permutation(own_key, shards_of)[partner]
    strong = (owner == chosen) | (owner == (partner + shards_of // 2) % shards_of)
    return jnp.where(strong, factor * values, values)


def shard_levels(own_key, dims, split, least, top_value):
    loudness, own = 1.0, jax.random.fold_in(own_key, 6)
    for position, blocks in split:
        draws = jnp.exp(jax.random.uniform(jax.random.fold_in(own, position), (blocks,), jnp.float32, least / len(split), top_value / len(split)))
        loudness = loudness * jnp.repeat(draws, dims[position] // blocks).reshape([-1 if axis == position else 1 for axis in range(len(dims))])
    return loudness


def noise(own_key, shape, deviation, bound, shards=(), held_as=jnp.bfloat16):
    factor_of = shard_levels(own_key, shape, shards, -0.22, 0.18) if shards else 1.0
    values = jax.random.normal(own_key, shape, jnp.float32) * deviation * factor_of
    return jnp.minimum(jnp.maximum(values, -bound), bound).astype(held_as)


def bell_draw_with(own_key, dims, scale, most, cuts, heavy, kind=jnp.bfloat16):
    values = scale * jax.random.normal(own_key, dims, jnp.float32)
    if cuts:
        values = values * shard_levels(own_key, dims, cuts, -0.22, 0.18)
    return jnp.clip(strengthened(values, jax.random.fold_in(own_key, 3), *heavy), -most, most).astype(kind)


def setup_inputs(seed: int = 0) -> dict:
    key_list = jax.random.split(jax.random.key(seed), 28)
    return {
        "acts": noise(key_list[0], (ALIGN, C, ROWS, D), 1.0, 6.0, ((0, 4), (1, 4), (2, 2))),
        "cotangent": bell_draw_with(key_list[1], (ALIGN, C, ROWS, D), 1.0, 8.0, ((0, 4), (1, 4), (2, 2)), (2, 3, 2, 2.0)),
        "col_mask": draw_col_mask(jax.random.fold_in(key_list[27], 71), 0),
        "ln_row_gain": jnp.clip(1.0 + 0.1 * jax.random.normal(key_list[3], (LAYERS, D), jnp.float32), 0.5, 1.5),
        "ln_row_bias": noise(key_list[4], (LAYERS, D), 0.2, 1.25, (), jnp.float32),
        "row_wq": noise(key_list[5], (LAYERS, D, D), D ** -0.5, 0.21875, ((2, 4),)),
        "row_wk": noise(key_list[6], (LAYERS, D, D), D ** -0.5, 0.21875, ((2, 4),)),
        "row_wv": noise(key_list[7], (LAYERS, D, D), D ** -0.5, 0.21875, ((2, 4),)),
        "row_bq": noise(key_list[8], (LAYERS, D), 0.2, 1.25, ((1, 4),), jnp.float32),
        "row_bv": noise(key_list[9], (LAYERS, D), 0.2, 1.25, ((1, 4),), jnp.float32),
        "row_wo": noise(key_list[10], (LAYERS, D, D), (D // 16) ** -0.5, 0.875, ((1, 4),)),
        "row_bo": noise(key_list[11], (LAYERS, D), 0.2, 1.25, (), jnp.float32),
        "ln_col_gain": jnp.clip(1.0 + 0.1 * jax.random.normal(key_list[12], (LAYERS, D), jnp.float32), 0.5, 1.5),
        "ln_col_bias": noise(key_list[13], (LAYERS, D), 0.2, 1.25, (), jnp.float32),
        "col_wq": noise(key_list[14], (LAYERS, D, D), D ** -0.5, 0.21875, ((2, 4),)),
        "col_wk": noise(key_list[15], (LAYERS, D, D), D ** -0.5, 0.21875, ((2, 4),)),
        "col_wv": noise(key_list[16], (LAYERS, D, D), D ** -0.5, 0.21875, ((2, 4),)),
        "col_bq": noise(key_list[17], (LAYERS, D), 0.2, 1.25, ((1, 4),), jnp.float32),
        "col_bv": noise(key_list[18], (LAYERS, D), 0.2, 1.25, ((1, 4),), jnp.float32),
        "col_wo": noise(key_list[19], (LAYERS, D, D), (D // 4) ** -0.5, 0.4375, ((1, 4),)),
        "col_bo": noise(key_list[20], (LAYERS, D), 0.2, 1.25, (), jnp.float32),
        "ln_ffn_gain": jnp.clip(1.0 + 0.1 * jax.random.normal(key_list[21], (LAYERS, D), jnp.float32), 0.5, 1.5),
        "ln_ffn_bias": noise(key_list[22], (LAYERS, D), 0.2, 1.25, (), jnp.float32),
        "ffn_w1": noise(key_list[23], (LAYERS, D, FF), D ** -0.5, 0.21875, ((2, 4),)),
        "ffn_b1": noise(key_list[24], (LAYERS, FF), 0.2, 1.25, ((1, 4),), jnp.float32),
        "ffn_w2": noise(key_list[25], (LAYERS, FF, D), (FF // 2) ** -0.5, 0.15625, ((1, 4),)),
        "ffn_b2": noise(key_list[26], (LAYERS, D), 0.2, 1.25, (), jnp.float32),
    }


@jax.custom_vjp
def low(v):
    return lax.optimization_barrier(v.astype(jnp.bfloat16)).astype(jnp.float32)

@jax.custom_vjp
def low_back(v):
    return v

def low_keep(v):
    return (low(v), None)

def low_pass(kept, grad):
    return (grad,)

def back_keep(v):
    return (v, None)

def back_low(kept, grad):
    return (low(grad),)
low.defvjp(low_keep, low_pass)
low_back.defvjp(back_keep, back_low)
PARAM_NAMES = ('ln_row_gain', 'ln_row_bias', 'row_wq', 'row_wk', 'row_wv', 'row_bq', 'row_bv', 'row_wo', 'row_bo', 'ln_col_gain', 'ln_col_bias', 'col_wq', 'col_wk', 'col_wv', 'col_bq', 'col_bv', 'col_wo', 'col_bo', 'ln_ffn_gain', 'ln_ffn_bias', 'ffn_w1', 'ffn_b1', 'ffn_w2', 'ffn_b2')

def einsum_high(pattern, first_operand, second_operand):
    return jnp.einsum(pattern, first_operand, second_operand, precision=lax.Precision.HIGHEST)

def layer_norm(values, norm_gain, norm_shift):
    average = lax.optimization_barrier(jnp.mean(values, axis=-1, keepdims=True))
    centred = values - average
    variance = lax.optimization_barrier(jnp.mean(centred * centred, axis=-1, keepdims=True))
    return centred * lax.rsqrt(variance + 1e-05) * norm_gain + norm_shift

def dense(values, weight):
    return einsum_high('crd,de->cre', values, weight)

def split_heads(values):
    return values.reshape(values.shape[:-1] + (values.shape[-1] // HD, HD))

def merge_heads(values):
    return values.reshape(values.shape[:-2] + (values.shape[-2] * values.shape[-1],))

def tied_rows(queries, key_rows, value_rows, valid_cols):
    columns = queries.shape[0]
    score_scale = 1.0 / math.sqrt(HD * queries.shape[1])
    block_cols = min(512, columns)
    live_keys = (valid_cols > 0)[None, None, :]

    def attend(query_block):
        logits = einsum_high('irhd,jrhd->ihj', query_block, key_rows)
        scores = jnp.where(live_keys, low_back(logits * score_scale), -1e+30)
        weights = low(jax.nn.softmax(scores, axis=-1))
        return einsum_high('ihj,jrhd->irhd', weights, value_rows)
    blocks = queries.reshape((columns // block_cols, block_cols) + queries.shape[1:])
    result = lax.map(jax.checkpoint(attend), blocks)
    return result.reshape(queries.shape)

def column_attend(queries, key_rows, value_rows):
    score_scale = 1.0 / math.sqrt(HD)
    scores = low_back(einsum_high('crhd,cshd->chrs', queries, key_rows) * score_scale)
    weights = low(jax.nn.softmax(scores, axis=-1))
    return einsum_high('chrs,cshd->crhd', weights, value_rows)

def row_block(params, layer_index, stream, valid_cols):
    normed = low(layer_norm(stream, params['ln_row_gain'][layer_index], params['ln_row_bias'][layer_index]))
    queries = low(low_back(dense(normed, params['row_wq'][layer_index]) + params['row_bq'][layer_index]))
    key_rows = low(low_back(dense(normed, params['row_wk'][layer_index])))
    value_rows = low(low_back(dense(normed, params['row_wv'][layer_index]) + params['row_bv'][layer_index]))
    head_values = tied_rows(split_heads(queries), split_heads(key_rows), split_heads(value_rows), valid_cols)
    head_values = low(low_back(merge_heads(head_values)))
    return stream + low_back(dense(head_values, params['row_wo'][layer_index]) + params['row_bo'][layer_index])

def column_block(params, layer_index, stream):
    normed = low(layer_norm(stream, params['ln_col_gain'][layer_index], params['ln_col_bias'][layer_index]))
    queries = low(low_back(dense(normed, params['col_wq'][layer_index]) + params['col_bq'][layer_index]))
    key_rows = low(low_back(dense(normed, params['col_wk'][layer_index])))
    value_rows = low(low_back(dense(normed, params['col_wv'][layer_index]) + params['col_bv'][layer_index]))
    head_values = column_attend(split_heads(queries), split_heads(key_rows), split_heads(value_rows))
    head_values = low(low_back(merge_heads(head_values)))
    return stream + low_back(dense(head_values, params['col_wo'][layer_index]) + params['col_bo'][layer_index])

def ffn_block(params, layer_index, stream):
    normed = low(layer_norm(stream, params['ln_ffn_gain'][layer_index], params['ln_ffn_bias'][layer_index]))
    up_values = low_back(dense(normed, params['ffn_w1'][layer_index]) + params['ffn_b1'][layer_index])
    activated = low(jax.nn.gelu(up_values, approximate=False))
    return stream + low_back(dense(activated, params['ffn_w2'][layer_index]) + params['ffn_b2'][layer_index])

def alignment_forward(params, stream, valid_cols):
    for layer_index in range(LAYERS):
        stream = row_block(params, layer_index, stream, valid_cols)
        stream = column_block(params, layer_index, stream)
        stream = ffn_block(params, layer_index, stream)
    return stream

def reference(acts, cotangent, col_mask, ln_row_gain, ln_row_bias, row_wq, row_wk, row_wv, row_bq, row_bv, row_wo, row_bo, ln_col_gain, ln_col_bias, col_wq, col_wk, col_wv, col_bq, col_bv, col_wo, col_bo, ln_ffn_gain, ln_ffn_bias, ffn_w1, ffn_b1, ffn_w2, ffn_b2):
    arrays = (ln_row_gain, ln_row_bias, row_wq, row_wk, row_wv, row_bq, row_bv, row_wo, row_bo, ln_col_gain, ln_col_bias, col_wq, col_wk, col_wv, col_bq, col_bv, col_wo, col_bo, ln_ffn_gain, ln_ffn_bias, ffn_w1, ffn_b1, ffn_w2, ffn_b2)
    params = {param_name: param_array.astype(jnp.float32) for param_name, param_array in zip(PARAM_NAMES, arrays)}
    stream_in = acts.astype(jnp.float32)
    runner = jax.checkpoint(alignment_forward)

    def forward(weights, inputs):
        return lax.map(lambda item_pair: runner(weights, item_pair[0], item_pair[1]), (inputs, col_mask))
    result, pullback = jax.vjp(forward, params, stream_in)
    gradients, grad_acts = pullback(cotangent.astype(jnp.float32))
    return (result, grad_acts, gradients['ln_row_gain'], gradients['ln_row_bias'], gradients['row_wq'], gradients['row_wk'], gradients['row_wv'], gradients['row_bq'], gradients['row_bv'], gradients['row_wo'], gradients['row_bo'], gradients['ln_col_gain'], gradients['ln_col_bias'], gradients['col_wq'], gradients['col_wk'], gradients['col_wv'], gradients['col_bq'], gradients['col_bv'], gradients['col_wo'], gradients['col_bo'], gradients['ln_ffn_gain'], gradients['ln_ffn_bias'], gradients['ffn_w1'], gradients['ffn_b1'], gradients['ffn_w2'], gradients['ffn_b2'])
```

```python
import math

import jax
import jax.numpy as jnp
from jax import lax
from jax.sharding import PartitionSpec as P

HD = 64
DP, SEQ, MP = AXES = ("dp", "seq", "mp")


EPSILON = 1e-05


def cut_along(shard, dim, peers):
    before, after = (shard.shape[:dim], shard.shape[dim + 1 :])
    return jnp.moveaxis(shard.reshape(*before, peers, -1, *after), dim, 0)


def sent_and_summed(shard, axis, dim):
    blocks = cut_along(shard, dim, lax.axis_size(axis))
    arrived = lax.all_to_all(blocks, axis, split_axis=0, concat_axis=0, tiled=True)
    return arrived.astype(jnp.float32).sum(axis=0)


def in_one_piece(arrays, axis, dim, along):
    ends, at = ([], 0)
    for a in arrays[:-1]:
        at += a.shape[along]
        ends.append(at)
    both = jnp.concatenate(arrays, axis=along)
    return tuple(jnp.split(sent_and_summed(both, axis, dim), ends, axis=along))


def normalize(values, norm_gain, norm_shift):
    average = jnp.mean(values, axis=-1, keepdims=True)
    centred = values - average
    variance = jnp.mean(centred * centred, axis=-1, keepdims=True)
    return centred * lax.rsqrt(variance + EPSILON) * norm_gain + norm_shift


def exact_gelu(values):
    return jax.nn.gelu(values, approximate=False)


def split_heads(values):
    return values.reshape(values.shape[:-1] + (values.shape[-1] // HD, HD))


def merge_heads(values):
    return values.reshape(values.shape[:-2] + (values.shape[-2] * values.shape[-1],))


def project(operand, weight):
    return lax.dot_general(
        operand, weight, (((operand.ndim - 1,), (0,)), ((), ())), preferred_element_type=jnp.float32
    )


def project_back(operand, weight):
    return lax.dot_general(
        operand, weight, (((operand.ndim - 1,), (1,)), ((), ())), preferred_element_type=jnp.float32
    )


def weight_gradient(operand, gradient):
    flat_operand = operand.reshape(-1, operand.shape[-1])
    flat_gradient = gradient.reshape(-1, gradient.shape[-1])
    return lax.dot_general(
        flat_operand, flat_gradient, (((0,), (0,)), ((), ())), preferred_element_type=jnp.float32
    )


def token_total(gradient):
    return jnp.sum(gradient.astype(jnp.float32).reshape(-1, gradient.shape[-1]), axis=0)


def model_gather(values):
    return lax.all_gather(values, MP, axis=0, tiled=True)


def model_sum(operand_pairs, backward):
    running_total = None
    for operand, weight in operand_pairs:
        if backward:
            product = project_back(operand, weight)
        else:
            product = project(operand, weight)
        running_total = product if running_total is None else running_total + product
    return lax.psum_scatter(
        running_total.astype(jnp.bfloat16), MP, scatter_dimension=0, tiled=True
    ).astype(jnp.float32)


def to_columns(values):
    return lax.all_to_all(
        values.astype(jnp.bfloat16), SEQ, split_axis=0, concat_axis=1, tiled=True
    ).astype(values.dtype)


def to_rows(values):
    return lax.all_to_all(
        values.astype(jnp.bfloat16), SEQ, split_axis=1, concat_axis=0, tiled=True
    ).astype(values.dtype)


def to_query_share(values):
    return lax.all_to_all(values, SEQ, split_axis=0, concat_axis=1, tiled=True)


def masked_softmax(logits, valid_cols, score_scale):
    scores = jnp.where((valid_cols > 0)[None, None, :], logits * score_scale, -1e30)
    highest = jnp.max(scores, axis=-1, keepdims=True)
    powers = jnp.exp(scores - highest)
    return powers / jnp.sum(powers, axis=-1, keepdims=True)


def tied_scale(key_rows):
    return 1.0 / math.sqrt(HD * key_rows.shape[1] * lax.axis_size(SEQ))


def tied_forward(queries, key_rows, value_rows, valid_cols):
    score_scale = tied_scale(key_rows)
    value_all = None
    key_all, value_all = (
        lax.all_gather(key_rows, SEQ, axis=1, tiled=True),
        lax.all_gather(value_rows, SEQ, axis=1, tiled=True),
    )
    query_share = to_query_share(queries)
    logits = jnp.einsum(
        "irhd,jrhd->hij",
        split_heads(query_share),
        split_heads(key_all),
        preferred_element_type=jnp.float32,
    )
    attention = masked_softmax(logits, valid_cols, score_scale)
    attention_all = lax.all_gather(attention.astype(jnp.bfloat16), SEQ, axis=1, tiled=True)
    head_values = jnp.einsum(
        "hij,jrhd->irhd", attention_all, split_heads(value_rows), preferred_element_type=jnp.float32
    )
    return (merge_heads(head_values).astype(jnp.bfloat16), attention, attention_all, value_all)


def tied_backward(grad_heads, queries, key_rows, attention, attention_all, value_all):
    score_scale = tied_scale(key_rows)
    grad_share = to_query_share(grad_heads)
    grad_weights = jnp.einsum(
        "irhd,jrhd->hij",
        split_heads(grad_share),
        split_heads(value_all),
        preferred_element_type=jnp.float32,
    )
    inner_sum = jnp.sum(attention * grad_weights, axis=-1, keepdims=True)
    grad_logits = (attention * (grad_weights - inner_sum)).astype(jnp.bfloat16)
    logits_all = lax.all_gather(grad_logits, SEQ, axis=1, tiled=True)
    grad_query = (
        jnp.einsum(
            "hij,jrhd->irhd", logits_all, split_heads(key_rows), preferred_element_type=jnp.float32
        )
        * score_scale
    )
    grad_key = (
        jnp.einsum(
            "hij,irhd->jrhd", logits_all, split_heads(queries), preferred_element_type=jnp.float32
        )
        * score_scale
    )
    grad_value = jnp.einsum(
        "hij,irhd->jrhd", attention_all, split_heads(grad_heads), preferred_element_type=jnp.float32
    )
    return (
        merge_heads(grad_query).astype(jnp.bfloat16),
        merge_heads(grad_key).astype(jnp.bfloat16),
        merge_heads(grad_value).astype(jnp.bfloat16),
    )


def column_forward(queries, key_rows, value_rows):
    score_scale = 1.0 / math.sqrt(HD)
    scores = (
        jnp.einsum(
            "crhd,cshd->chrs",
            split_heads(queries),
            split_heads(key_rows),
            preferred_element_type=jnp.float32,
        )
        * score_scale
    )
    highest = jnp.max(scores, axis=-1, keepdims=True)
    powers = jnp.exp(scores - highest)
    attention = powers / jnp.sum(powers, axis=-1, keepdims=True)
    attention_low = attention.astype(jnp.bfloat16)
    head_values = jnp.einsum(
        "chrs,cshd->crhd",
        attention_low,
        split_heads(value_rows),
        preferred_element_type=jnp.float32,
    )
    return (merge_heads(head_values).astype(jnp.bfloat16), attention, attention_low)


def column_backward(grad_heads, queries, key_rows, value_rows, attention, attention_low):
    score_scale = 1.0 / math.sqrt(HD)
    grad_split = split_heads(grad_heads)
    grad_weights = jnp.einsum(
        "crhd,cshd->chrs", grad_split, split_heads(value_rows), preferred_element_type=jnp.float32
    )
    grad_value = jnp.einsum(
        "chrs,crhd->cshd", attention_low, grad_split, preferred_element_type=jnp.float32
    )
    inner_sum = jnp.sum(attention * grad_weights, axis=-1, keepdims=True)
    grad_logits = (attention * (grad_weights - inner_sum)).astype(jnp.bfloat16)
    grad_query = (
        jnp.einsum(
            "chrs,cshd->crhd",
            grad_logits,
            split_heads(key_rows),
            preferred_element_type=jnp.float32,
        )
        * score_scale
    )
    grad_key = (
        jnp.einsum(
            "chrs,crhd->cshd", grad_logits, split_heads(queries), preferred_element_type=jnp.float32
        )
        * score_scale
    )
    return (
        merge_heads(grad_query).astype(jnp.bfloat16),
        merge_heads(grad_key).astype(jnp.bfloat16),
        merge_heads(grad_value).astype(jnp.bfloat16),
    )


def norm_backward(values, norm_gain, norm_shift, gradient):
    norm_value, norm_pull = jax.vjp(normalize, values, norm_gain, norm_shift)
    return norm_pull(gradient)


def on_device(
    acts,
    cotangent,
    col_mask,
    ln_row_gain,
    ln_row_bias,
    row_wq,
    row_wk,
    row_wv,
    row_bq,
    row_bv,
    row_wo,
    row_bo,
    ln_col_gain,
    ln_col_bias,
    col_wq,
    col_wk,
    col_wv,
    col_bq,
    col_bv,
    col_wo,
    col_bo,
    ln_ffn_gain,
    ln_ffn_bias,
    ffn_w1,
    ffn_b1,
    ffn_w2,
    ffn_b2,
):
    stream = acts[0].astype(jnp.float32)
    valid_cols = col_mask[0]
    rec_row_in = stream
    normed = normalize(stream, ln_row_gain[0], ln_row_bias[0]).astype(
        jnp.bfloat16
    )
    hidden = model_gather(normed)
    queries = (project(hidden, row_wq[0]) + row_bq[0]).astype(jnp.bfloat16)
    key_rows = project(hidden, row_wk[0]).astype(jnp.bfloat16)
    value_rows = (project(hidden, row_wv[0]) + row_bv[0]).astype(jnp.bfloat16)
    head_values, attention, attention_all, value_all = tied_forward(
        queries, key_rows, value_rows, valid_cols
    )
    stream = stream + model_sum(((head_values, row_wo[0]),), False) + row_bo[0]
    rec_row_hidden = hidden
    rec_row_queries = queries
    rec_row_keys = key_rows
    rec_row_values = value_rows
    rec_row_attention = attention
    rec_row_attention_all = attention_all
    rec_row_value_all = value_all
    rec_row_heads = head_values
    column_stream = to_columns(stream)
    rec_col_in = column_stream
    normed = normalize(column_stream, ln_col_gain[0], ln_col_bias[0]).astype(
        jnp.bfloat16
    )
    hidden = model_gather(normed)
    queries = (project(hidden, col_wq[0]) + col_bq[0]).astype(jnp.bfloat16)
    key_rows = project(hidden, col_wk[0]).astype(jnp.bfloat16)
    value_rows = (project(hidden, col_wv[0]) + col_bv[0]).astype(jnp.bfloat16)
    head_values, attention, attention_low = column_forward(queries, key_rows, value_rows)
    column_stream = (
        column_stream
        + model_sum(((head_values, col_wo[0]),), False)
        + col_bo[0]
    )
    rec_col_hidden = hidden
    rec_col_queries = queries
    rec_col_keys = key_rows
    rec_col_values = value_rows
    rec_col_attention = attention
    rec_col_attention_low = attention_low
    rec_col_heads = head_values
    rec_ffn_in = column_stream
    normed = normalize(column_stream, ln_ffn_gain[0], ln_ffn_bias[0]).astype(
        jnp.bfloat16
    )
    hidden = model_gather(normed)
    up_values = project(hidden, ffn_w1[0]) + ffn_b1[0]
    activated = exact_gelu(up_values).astype(jnp.bfloat16)
    column_stream = (
        column_stream + model_sum(((activated, ffn_w2[0]),), False) + ffn_b2[0]
    )
    rec_ffn_hidden = hidden
    rec_ffn_up = up_values
    rec_ffn_act = activated
    stream = to_rows(column_stream)
    gradient = cotangent[0].astype(jnp.float32)
    column_grad = to_columns(gradient)
    grad_low = column_grad.astype(jnp.bfloat16)
    grad_all = model_gather(grad_low)
    g_ffn_w2 = weight_gradient(rec_ffn_act, grad_all)
    g_ffn_b2 = token_total(grad_low)
    grad_act = project_back(grad_all, ffn_w2[0])
    gelu_value, gelu_pull = jax.vjp(exact_gelu, rec_ffn_up)
    grad_up = gelu_pull(grad_act)[0].astype(jnp.bfloat16)
    g_ffn_w1 = weight_gradient(rec_ffn_hidden, grad_up)
    g_ffn_b1 = token_total(grad_up)
    grad_normed = model_sum(((grad_up, ffn_w1[0]),), True)
    grad_input, grad_gain, grad_shift = norm_backward(
        rec_ffn_in, ln_ffn_gain[0], ln_ffn_bias[0], grad_normed
    )
    g_ln_ffn_gain = grad_gain
    g_ln_ffn_bias = grad_shift
    column_grad = column_grad + grad_input
    grad_low = column_grad.astype(jnp.bfloat16)
    grad_all = model_gather(grad_low)
    g_col_wo = weight_gradient(rec_col_heads, grad_all)
    g_col_bo = token_total(grad_low)
    grad_heads = project_back(grad_all, col_wo[0]).astype(jnp.bfloat16)
    grad_query, grad_key, grad_value = column_backward(
        grad_heads,
        rec_col_queries,
        rec_col_keys,
        rec_col_values,
        rec_col_attention,
        rec_col_attention_low,
    )
    g_col_wq = weight_gradient(rec_col_hidden, grad_query)
    g_col_wk = weight_gradient(rec_col_hidden, grad_key)
    g_col_wv = weight_gradient(rec_col_hidden, grad_value)
    g_col_bq = token_total(grad_query)
    g_col_bv = token_total(grad_value)
    grad_normed = model_sum(
        (
            (grad_query, col_wq[0]),
            (grad_key, col_wk[0]),
            (grad_value, col_wv[0]),
        ),
        True,
    )
    grad_input, grad_gain, grad_shift = norm_backward(
        rec_col_in, ln_col_gain[0], ln_col_bias[0], grad_normed
    )
    g_ln_col_gain = grad_gain
    g_ln_col_bias = grad_shift
    column_grad = column_grad + grad_input
    gradient = to_rows(column_grad)
    grad_low = gradient.astype(jnp.bfloat16)
    grad_all = model_gather(grad_low)
    g_row_wo = weight_gradient(rec_row_heads, grad_all)
    g_row_bo = token_total(grad_low)
    grad_heads = project_back(grad_all, row_wo[0]).astype(jnp.bfloat16)
    grad_query, grad_key, grad_value = tied_backward(
        grad_heads,
        rec_row_queries,
        rec_row_keys,
        rec_row_attention,
        rec_row_attention_all,
        rec_row_value_all,
    )
    g_row_wq = weight_gradient(rec_row_hidden, grad_query)
    g_row_wk = weight_gradient(rec_row_hidden, grad_key)
    g_row_wv = weight_gradient(rec_row_hidden, grad_value)
    g_row_bq = token_total(grad_query)
    g_row_bv = token_total(grad_value)
    grad_normed = model_sum(
        (
            (grad_query, row_wq[0]),
            (grad_key, row_wk[0]),
            (grad_value, row_wv[0]),
        ),
        True,
    )
    grad_input, grad_gain, grad_shift = norm_backward(
        rec_row_in, ln_row_gain[0], ln_row_bias[0], grad_normed
    )
    g_ln_row_gain = grad_gain
    g_ln_row_bias = grad_shift
    gradient = gradient + grad_input
    matrix_totals = (
        lax.psum_scatter(
            g_row_wq[None], (DP, SEQ), scatter_dimension=1, tiled=True
        ),
        lax.psum_scatter(
            g_row_wk[None], (DP, SEQ), scatter_dimension=1, tiled=True
        ),
        lax.psum_scatter(
            g_row_wv[None], (DP, SEQ), scatter_dimension=1, tiled=True
        ),
        lax.psum_scatter(
            g_col_wq[None], (DP, SEQ), scatter_dimension=1, tiled=True
        ),
        lax.psum_scatter(
            g_col_wk[None], (DP, SEQ), scatter_dimension=1, tiled=True
        ),
        lax.psum_scatter(
            g_col_wv[None], (DP, SEQ), scatter_dimension=1, tiled=True
        ),
        lax.psum_scatter(
            g_ffn_w1[None], (DP, SEQ), scatter_dimension=1, tiled=True
        ),
    )
    output_totals = in_one_piece(
        (
            g_row_wo[None].astype(jnp.bfloat16),
            g_col_wo[None].astype(jnp.bfloat16),
            g_ffn_w2[None].astype(jnp.bfloat16),
        ),
        (DP, SEQ),
        2,
        1,
    )
    vector_totals = (
        lax.psum_scatter(
            g_ln_row_gain[None],
            (DP, SEQ, MP),
            scatter_dimension=1,
            tiled=True,
        ),
        lax.psum_scatter(
            g_ln_row_bias[None],
            (DP, SEQ, MP),
            scatter_dimension=1,
            tiled=True,
        ),
        lax.psum_scatter(
            g_row_bo[None], (DP, SEQ, MP), scatter_dimension=1, tiled=True
        ),
        lax.psum_scatter(
            g_ln_col_gain[None],
            (DP, SEQ, MP),
            scatter_dimension=1,
            tiled=True,
        ),
        lax.psum_scatter(
            g_ln_col_bias[None],
            (DP, SEQ, MP),
            scatter_dimension=1,
            tiled=True,
        ),
        lax.psum_scatter(
            g_col_bo[None], (DP, SEQ, MP), scatter_dimension=1, tiled=True
        ),
        lax.psum_scatter(
            g_ln_ffn_gain[None],
            (DP, SEQ, MP),
            scatter_dimension=1,
            tiled=True,
        ),
        lax.psum_scatter(
            g_ln_ffn_bias[None],
            (DP, SEQ, MP),
            scatter_dimension=1,
            tiled=True,
        ),
        lax.psum_scatter(
            g_ffn_b2[None], (DP, SEQ, MP), scatter_dimension=1, tiled=True
        ),
    )
    bias_totals = lax.psum(
        (
            g_row_bq[None],
            g_row_bv[None],
            g_col_bq[None],
            g_col_bv[None],
            g_ffn_b1[None],
        ),
        (DP, SEQ),
    )
    return (
        stream[None],
        gradient[None],
        vector_totals[0],
        vector_totals[1],
        matrix_totals[0],
        matrix_totals[1],
        matrix_totals[2],
        bias_totals[0],
        bias_totals[1],
        output_totals[0],
        vector_totals[2],
        vector_totals[3],
        vector_totals[4],
        matrix_totals[3],
        matrix_totals[4],
        matrix_totals[5],
        bias_totals[2],
        bias_totals[3],
        output_totals[1],
        vector_totals[5],
        vector_totals[6],
        vector_totals[7],
        matrix_totals[6],
        bias_totals[4],
        output_totals[2],
        vector_totals[8],
    )


def routed(values, target_of):
    dps, seqs, mps = (lax.axis_size(axis) for axis in AXES)
    pairs = []
    for d in range(dps):
        for s in range(seqs):
            for m in range(mps):
                to_d, to_s, to_m = target_of(d, s, m)
                pairs.append(((d * seqs + s) * mps + m, (to_d * seqs + to_s) * mps + to_m))
    return lax.ppermute(values, AXES, pairs)


def shifted(values, step):
    mps = lax.axis_size(MP)
    return routed(values, lambda d, s, m: (d, s, (m + step) % mps))


def to_sibling(values):
    return routed(values, lambda d, s, m: (d ^ 1, s, m))


def straight(d, s, m):
    return (d // 2 * 2 + s, d % 2, m)


def crossed(d, s, m):
    return (d // 2 * 2 + 1 - s, d % 2, m)


def crossed_back(d, s, m):
    return (d // 2 * 2 + s, 1 - d % 2, m)


def to_work(values):
    half = values.shape[0] // 2
    x = lax.axis_index(SEQ)
    mine = lax.dynamic_slice_in_dim(values, x * half, half, axis=0)
    other = lax.dynamic_slice_in_dim(values, (1 - x) * half, half, axis=0)
    return jnp.stack([routed(mine, straight), routed(other, crossed)])


def from_work(values):
    x = lax.axis_index(SEQ)
    mine, other = routed(values[0], straight), routed(values[1], crossed_back)
    halves = jnp.stack([jnp.where(x == 0, mine, other), jnp.where(x == 0, other, mine)])
    return halves.reshape(-1, halves.shape[-1])


def dot(a, b, dims):
    return lax.dot_general(a, b, (dims, ((), ())), preferred_element_type=jnp.float32)


def low(values):
    return values.astype(jnp.bfloat16)


def norm_parts(values):
    average = jnp.mean(values, axis=-1, keepdims=True)
    centred = values - average
    scale = lax.rsqrt(jnp.mean(centred * centred, axis=-1, keepdims=True) + EPSILON)
    return centred * scale, scale


def norm_pull(unit, scale, norm_gain, gradient):
    q = gradient * norm_gain
    return (
        q - jnp.mean(q, axis=-1, keepdims=True) - unit * jnp.mean(q * unit, axis=-1, keepdims=True)
    ) * scale


def all_tokens(values):
    return values.reshape(-1, values.shape[-1])


def total(values):
    return jnp.sum(values.astype(jnp.float32).reshape(-1, values.shape[-1]), axis=0)


def on_device_columns(
    acts,
    cotangent,
    col_mask,
    ln_row_gain,
    ln_row_bias,
    row_wq,
    row_wk,
    row_wv,
    row_bq,
    row_bv,
    row_wo,
    row_bo,
    ln_col_gain,
    ln_col_bias,
    col_wq,
    col_wk,
    col_wv,
    col_bq,
    col_bv,
    col_wo,
    col_bo,
    ln_ffn_gain,
    ln_ffn_bias,
    ffn_w1,
    ffn_b1,
    ffn_w2,
    ffn_b2,
):
    width = acts.shape[-1]
    hs = row_wq.shape[2]
    heads = hs // HD
    fs = ffn_w1.shape[2]
    ranks = lax.axis_size(DP) * lax.axis_size(SEQ)
    mps = lax.axis_size(MP)
    rank = lax.axis_index(DP) * lax.axis_size(SEQ) + lax.axis_index(SEQ)
    c, z = lax.axis_index(DP) % 2, lax.axis_index(MP)
    ch, fh, dh = hs // ranks, fs // ranks, width // ranks

    stream = to_work(acts[0, :, 0]).astype(jnp.float32)
    mask = routed(col_mask[0], straight)
    half = stream.shape[1]

    def share(matrix, rows):
        return lax.dynamic_slice_in_dim(matrix, rank * rows, rows, axis=0)

    col_q_t, col_k_t, col_v_t = col_wq[0].T, col_wk[0].T, col_wv[0].T

    def two_parts(v):
        upper = low(v)
        return upper, low(v - upper.astype(jnp.float32))

    b1_parts, bq_parts, bv_parts = two_parts(ffn_b1[0]), two_parts(col_bq[0]), two_parts(col_bv[0])
    bias_rows = jnp.concatenate(
        [
            jnp.stack(b1_parts),
            jnp.concatenate(bq_parts + bv_parts)[None],
            jnp.zeros((5, width), jnp.bfloat16),
        ]
    )
    pack_attention = jnp.concatenate(
        [share(w, ch) for w in (col_q_t, col_k_t, col_v_t, col_wo[0], row_wo[0])] + [bias_rows]
    )
    pack_ffn = jnp.concatenate([share(ffn_w1[0], dh), share(ffn_w2[0], fh)])

    def gathered(pack):
        away = jnp.stack([shifted(pack, k) for k in range(1, mps)])
        return away, lax.all_gather(away, (DP, SEQ), axis=0, tiled=False)

    away_attention, whole_attention = gathered(pack_attention)
    away_ffn, whole_ffn = gathered(pack_ffn)

    def full_rows(own, whole, at, rows):
        rest = whole[:, :, at : at + rows].swapaxes(0, 1).reshape(mps - 1, ranks * rows, width)
        return jnp.concatenate([own[None], rest])

    wq_t = full_rows(col_q_t, whole_attention, 0, ch).reshape(-1, width)
    wk_t = full_rows(col_k_t, whole_attention, ch, ch).reshape(-1, width)
    wv_t = full_rows(col_v_t, whole_attention, 2 * ch, ch).reshape(-1, width)
    col_o = full_rows(col_wo[0], whole_attention, 3 * ch, ch).reshape(-1, width)
    row_o = full_rows(row_wo[0], whole_attention, 4 * ch, ch).reshape(-1, width)
    w1 = full_rows(ffn_w1[0], whole_ffn, 0, dh)
    w2 = full_rows(ffn_w2[0], whole_ffn, dh, fh).reshape(-1, width)
    bias_away = away_attention[:, 5 * ch :].astype(jnp.float32)
    b1 = jnp.concatenate([ffn_b1[0]] + [bias_away[k, 0] + bias_away[k, 1] for k in range(mps - 1)])
    bq = jnp.concatenate(
        [col_bq[0]]
        + [bias_away[k, 2, :hs] + bias_away[k, 2, hs : 2 * hs] for k in range(mps - 1)]
    )
    bv = jnp.concatenate(
        [col_bv[0]]
        + [
            bias_away[k, 2, 2 * hs : 3 * hs] + bias_away[k, 2, 3 * hs : 4 * hs]
            for k in range(mps - 1)
        ]
    )

    row_unit, row_scale = norm_parts(stream)
    normed = low(row_unit * ln_row_gain[0] + ln_row_bias[0])
    hidden = jnp.stack([normed] + [shifted(normed, k) for k in range(1, mps)])
    row_w = jnp.concatenate([row_wq[0], row_wk[0], row_wv[0]], axis=1)
    row_b = jnp.concatenate([row_bq[0], jnp.zeros_like(row_bq[0]), row_bv[0]])
    qkv = low(dot(hidden, row_w, ((3,), (0,))) + row_b)
    kv_sibling = to_sibling(qkv[:, ::-1, :, hs:])
    block = 2 * half

    def by_head(v):
        v = v.reshape(mps, 2, half, heads, HD)
        return v.transpose(3, 0, 2, 1, 4).reshape(heads, mps * half, 2 * HD)

    def from_head(v):
        v = v.reshape(heads, mps, half, 2, HD)
        return v.transpose(1, 3, 2, 0, 4).reshape(mps, 2, half, hs)

    q_h = by_head(qkv[..., :hs])
    k_h = jnp.concatenate([by_head(qkv[..., hs : 2 * hs]), by_head(kv_sibling[..., :hs])], axis=1)
    v_h = jnp.concatenate([by_head(qkv[..., 2 * hs :]), by_head(kv_sibling[..., hs:])], axis=1)
    score_scale = 1.0 / math.sqrt(HD * 2)
    mask_blocks = mask.reshape(mps, 2, half)
    mask_near = jnp.stack(
        [
            lax.dynamic_index_in_dim(mask_blocks, (z - k) % mps, keepdims=False)
            for k in range(mps)
        ],
        axis=1,
    )
    mask_near = jnp.where(c == 0, mask_near, mask_near[::-1])
    logits = jnp.einsum("hid,hjd->hij", q_h, k_h, preferred_element_type=jnp.float32)
    attention = masked_softmax(logits, mask_near.reshape(-1), score_scale)
    attention_low = low(attention)
    o_h = jnp.einsum("hij,hjd->hid", attention_low, v_h, preferred_element_type=jnp.float32)
    o_blocks = from_head(low(o_h))
    o_from = [o_blocks[0]] + [shifted(o_blocks[k], -k) for k in range(1, mps)]
    row_heads = jnp.concatenate([o_from[-k % mps] for k in range(mps)], axis=-1)
    stream = stream + dot(row_heads, row_o, ((2,), (0,))) + row_bo[0]

    col_unit, col_scale = norm_parts(stream)
    col_normed = low(col_unit * ln_col_gain[0] + ln_col_bias[0])
    col_q = low(dot(col_normed, wq_t, ((2,), (1,))) + bq)
    col_k = low(dot(col_normed, wk_t, ((2,), (1,))))
    col_v = low(dot(col_normed, wv_t, ((2,), (1,))) + bv)
    col_scale_factor = 1.0 / math.sqrt(HD)

    def head_sums(a, b):
        product = a.astype(jnp.float32) * b.astype(jnp.float32)
        return product.reshape(half, mps * heads, HD).sum(axis=-1)

    def spread(v):
        return jnp.repeat(v, HD, axis=-1)

    def pair_softmax(r):
        a = head_sums(col_q[r], col_k[0]) * col_scale_factor
        b = head_sums(col_q[r], col_k[1]) * col_scale_factor
        highest = jnp.maximum(a, b)
        ea, eb = jnp.exp(a - highest), jnp.exp(b - highest)
        return ea / (ea + eb), eb / (ea + eb)

    col_attention = [pair_softmax(r) for r in range(2)]
    value32 = col_v.astype(jnp.float32)
    weight_low = [
        [spread(low(col_attention[r][s]).astype(jnp.float32)) for s in range(2)] for r in range(2)
    ]
    col_heads = low(
        jnp.stack(
            [weight_low[r][0] * value32[0] + weight_low[r][1] * value32[1] for r in range(2)]
        )
    )
    col_stream = stream + dot(col_heads, col_o, ((2,), (0,))) + col_bo[0]

    ffn_unit, ffn_scale = norm_parts(col_stream)
    ffn_normed = low(ffn_unit * ln_ffn_gain[0] + ln_ffn_bias[0])
    up = jnp.concatenate([dot(ffn_normed, w1[k], ((2,), (0,))) for k in range(mps)], axis=-1) + b1
    activated, gelu_pull = jax.vjp(exact_gelu, up)
    activated = low(activated)
    out_stream = col_stream + dot(activated, w2, ((2,), (0,))) + ffn_b2[0]
    out = from_work(low(out_stream)).astype(jnp.float32)

    grad_low = to_work(cotangent[0, :, 0])
    gradient = grad_low.astype(jnp.float32)
    grad_b2 = total(grad_low)
    grad_up = low(gelu_pull(dot(grad_low, w2, ((2,), (1,))))[0])
    grad_b1 = total(grad_up)
    grad_normed = sum(
        dot(grad_up[..., k * fs : (k + 1) * fs], w1[k], ((2,), (1,))) for k in range(mps)
    )
    grad_ln_ffn_gain, grad_ln_ffn_bias = total(grad_normed * ffn_unit), total(grad_normed)
    token_dims = ((0,), (0,))
    grad_ffn = jnp.stack(
        [
            low(dot(all_tokens(ffn_normed), all_tokens(grad_up), token_dims)),
            low(dot(all_tokens(grad_low), all_tokens(activated), token_dims)),
        ],
        axis=1,
    )
    gradient = gradient + norm_pull(ffn_unit, ffn_scale, ln_ffn_gain[0], grad_normed)

    grad_low = low(gradient)
    grad_col_bo = total(grad_low)
    grad_heads = low(dot(grad_low, col_o, ((2,), (1,))))
    grad32 = grad_heads.astype(jnp.float32)
    grad_logits = []
    for r in range(2):
        parts = [head_sums(grad_heads[r], col_v[s]) for s in range(2)]
        inner = col_attention[r][0] * parts[0] + col_attention[r][1] * parts[1]
        grad_logits.append(
            [
                spread(low(col_attention[r][s] * (parts[s] - inner)).astype(jnp.float32))
                for s in range(2)
            ]
        )
    q32, k32 = col_q.astype(jnp.float32), col_k.astype(jnp.float32)
    grad_q = low(
        jnp.stack(
            [
                (grad_logits[r][0] * k32[0] + grad_logits[r][1] * k32[1]) * col_scale_factor
                for r in range(2)
            ]
        )
    )
    grad_k = low(
        jnp.stack(
            [
                (grad_logits[0][s] * q32[0] + grad_logits[1][s] * q32[1]) * col_scale_factor
                for s in range(2)
            ]
        )
    )
    grad_v = low(
        jnp.stack([weight_low[0][s] * grad32[0] + weight_low[1][s] * grad32[1] for s in range(2)])
    )
    grad_col_bq, grad_col_bv = total(grad_q), total(grad_v)
    grad_normed = (
        dot(grad_q, wq_t, ((2,), (0,)))
        + dot(grad_k, wk_t, ((2,), (0,)))
        + dot(grad_v, wv_t, ((2,), (0,)))
    )
    grad_ln_col_gain, grad_ln_col_bias = total(grad_normed * col_unit), total(grad_normed)
    gradient = gradient + norm_pull(col_unit, col_scale, ln_col_gain[0], grad_normed)

    col_grad_low, grad_low = grad_low, low(gradient)
    grad_row_bo = total(grad_low)
    grad_heads = low(dot(grad_low, row_o, ((2,), (1,))))
    d_from = [grad_heads[..., :hs]] + [
        shifted(grad_heads[..., k * hs : (k + 1) * hs], -k) for k in range(1, mps)
    ]
    d_h = by_head(jnp.stack([d_from[-k % mps] for k in range(mps)]))
    normed_flat = all_tokens(col_normed)
    grad_attention = jnp.stack(
        [
            low(dot(normed_flat, all_tokens(g), token_dims)) for g in (grad_q, grad_k, grad_v)
        ]
        + [
            low(dot(all_tokens(col_grad_low), all_tokens(col_heads), token_dims)),
            low(dot(all_tokens(grad_low), all_tokens(row_heads), token_dims)),
        ],
        axis=1,
    )

    grad_weights = jnp.einsum("hid,hjd->hij", d_h, v_h, preferred_element_type=jnp.float32)
    inner = jnp.sum(attention * grad_weights, axis=-1, keepdims=True)
    grad_logits = low(attention * (grad_weights - inner))
    gq_h = (
        jnp.einsum("hij,hjd->hid", grad_logits, k_h, preferred_element_type=jnp.float32)
        * score_scale
    )
    gk_h = (
        jnp.einsum("hij,hid->hjd", grad_logits, q_h, preferred_element_type=jnp.float32)
        * score_scale
    )
    gv_h = jnp.einsum("hij,hid->hjd", attention_low, d_h, preferred_element_type=jnp.float32)
    keys = mps * half
    mine = jnp.concatenate([from_head(gk_h[:, :keys]), from_head(gv_h[:, :keys])], axis=-1)
    theirs = jnp.concatenate([from_head(gk_h[:, keys:]), from_head(gv_h[:, keys:])], axis=-1)
    g_kv = low(mine + to_sibling(low(theirs[:, ::-1])).astype(jnp.float32))
    g_qkv = jnp.concatenate([low(from_head(gq_h)), g_kv], axis=-1)
    g_hidden = dot(g_qkv, row_w, ((3,), (1,)))
    g_send = low(g_hidden)
    g_parts = [g_send[0]] + [shifted(g_send[k], -k) for k in range(1, mps)]
    grad_normed = sum(g.astype(jnp.float32) for g in g_parts)
    gradient = gradient + norm_pull(row_unit, row_scale, ln_row_gain[0], grad_normed)
    grad_acts = from_work(low(gradient)).astype(jnp.float32)
    grad_row_qkv = low(dot(all_tokens(hidden), all_tokens(g_qkv), token_dims))

    rank_axes = (DP, SEQ)

    def reduced(parts):
        mine = lax.psum_scatter(parts, rank_axes, scatter_dimension=0, tiled=True)
        size = mine.shape[-1] // mps
        pieces = [mine[..., :size]] + [
            shifted(mine[..., k * size : (k + 1) * size], -k) for k in range(1, mps)
        ]
        return sum(p.astype(jnp.float32) for p in pieces)

    ffn_total = reduced(grad_ffn)
    attention_total = reduced(grad_attention)
    row_total = lax.psum_scatter(
        grad_row_qkv, rank_axes, scatter_dimension=0, tiled=True
    ).astype(jnp.float32)

    row_hidden_unit = (hidden.astype(jnp.float32) - ln_row_bias[0]) / ln_row_gain[0]
    grad_ln_row_gain, grad_ln_row_bias = total(g_hidden * row_hidden_unit), total(g_hidden)
    here = (jnp.arange(mps) == z).astype(jnp.float32)[:, None]

    def by_shard(v):
        v = v.reshape(mps, -1)
        near = (z - jnp.arange(mps)) % mps
        return sum(
            jnp.where((near[k] == jnp.arange(mps))[:, None], v[k], 0.0) for k in range(mps)
        ).reshape(-1)

    row_bias = [
        (here * total(g_qkv[..., :hs])).reshape(-1),
        (here * total(g_qkv[..., 2 * hs :])).reshape(-1),
    ]
    summed = lax.psum(
        jnp.concatenate(
            [
                grad_ln_row_gain,
                grad_ln_row_bias,
                grad_row_bo,
                grad_ln_col_gain,
                grad_ln_col_bias,
                grad_col_bo,
                grad_ln_ffn_gain,
                grad_ln_ffn_bias,
                grad_b2,
            ]
            + row_bias
            + [by_shard(grad_col_bq), by_shard(grad_col_bv), by_shard(grad_b1)]
        ),
        AXES,
    )
    device = rank * mps + z
    vectors = summed[: 9 * width].reshape(9, ranks * mps, -1)
    vectors = lax.dynamic_index_in_dim(vectors, device, axis=1, keepdims=False)
    biases = summed[9 * width :]

    def of_shard(at, size):
        return lax.dynamic_slice_in_dim(biases[at : at + mps * size], z * size, size)[None]

    def transposed(v):
        return v.T[None]

    return (
        out[None, :, None],
        grad_acts[None, :, None],
        vectors[0][None],
        vectors[1][None],
        row_total[:, :hs][None],
        row_total[:, hs : 2 * hs][None],
        row_total[:, 2 * hs :][None],
        of_shard(0, hs),
        of_shard(width, hs),
        transposed(attention_total[:, 4]),
        vectors[2][None],
        vectors[3][None],
        vectors[4][None],
        attention_total[:, 0][None],
        attention_total[:, 1][None],
        attention_total[:, 2][None],
        of_shard(2 * width, hs),
        of_shard(3 * width, hs),
        transposed(attention_total[:, 3]),
        vectors[5][None],
        vectors[6][None],
        vectors[7][None],
        ffn_total[:, 0][None],
        of_shard(4 * width, fs),
        transposed(ffn_total[:, 1]),
        vectors[8][None],
    )


def solution(mesh):
    placed = (
        P(DP, MP, SEQ, None),
        P(DP, MP, SEQ, None),
        P(DP, None),
        P(),
        P(),
        P(None, None, MP),
        P(None, None, MP),
        P(None, None, MP),
        P(None, MP),
        P(None, MP),
        P(None, MP, None),
        P(),
        P(),
        P(),
        P(None, None, MP),
        P(None, None, MP),
        P(None, None, MP),
        P(None, MP),
        P(None, MP),
        P(None, MP, None),
        P(),
        P(),
        P(),
        P(None, None, MP),
        P(None, MP),
        P(None, MP, None),
        P(),
    )
    in_pairs = mesh.shape[SEQ] == 2 and mesh.shape[DP] % 2 == 0
    return jax.shard_map(
        on_device_columns if in_pairs else on_device,
        mesh=mesh,
        in_specs=placed,
        out_specs=(
            P(DP, MP, SEQ, None),
            P(DP, MP, SEQ, None),
            P(None, (DP, SEQ, MP)),
            P(None, (DP, SEQ, MP)),
            P(None, (DP, SEQ), MP),
            P(None, (DP, SEQ), MP),
            P(None, (DP, SEQ), MP),
            P(None, MP),
            P(None, MP),
            P(None, MP, (DP, SEQ)),
            P(None, (DP, SEQ, MP)),
            P(None, (DP, SEQ, MP)),
            P(None, (DP, SEQ, MP)),
            P(None, (DP, SEQ), MP),
            P(None, (DP, SEQ), MP),
            P(None, (DP, SEQ), MP),
            P(None, MP),
            P(None, MP),
            P(None, MP, (DP, SEQ)),
            P(None, (DP, SEQ, MP)),
            P(None, (DP, SEQ, MP)),
            P(None, (DP, SEQ, MP)),
            P(None, (DP, SEQ), MP),
            P(None, MP),
            P(None, MP, (DP, SEQ)),
            P(None, (DP, SEQ, MP)),
        ),
        check_vma=False,
    )
```

```python
import functools
import math

import jax
import jax.numpy as jnp
from jax import lax
from jax.experimental import pallas as pl
from jax.experimental.pallas import tpu as pltpu
from jax.sharding import PartitionSpec as P

HD = 64
DP, SEQ, MP = AXES = ("dp", "seq", "mp")


EPSILON = 1e-05


def cut_along(shard, dim, peers):
    before, after = (shard.shape[:dim], shard.shape[dim + 1 :])
    return jnp.moveaxis(shard.reshape(*before, peers, -1, *after), dim, 0)


def sent_and_summed(shard, axis, dim):
    blocks = cut_along(shard, dim, lax.axis_size(axis))
    arrived = lax.all_to_all(blocks, axis, split_axis=0, concat_axis=0, tiled=True)
    return arrived.astype(jnp.float32).sum(axis=0)


def in_one_piece(arrays, axis, dim, along):
    ends, at = ([], 0)
    for a in arrays[:-1]:
        at += a.shape[along]
        ends.append(at)
    both = jnp.concatenate(arrays, axis=along)
    return tuple(jnp.split(sent_and_summed(both, axis, dim), ends, axis=along))


def normalize(values, norm_gain, norm_shift):
    average = jnp.mean(values, axis=-1, keepdims=True)
    centred = values - average
    variance = jnp.mean(centred * centred, axis=-1, keepdims=True)
    return centred * lax.rsqrt(variance + EPSILON) * norm_gain + norm_shift


def exact_gelu(values):
    return jax.nn.gelu(values, approximate=False)


def split_heads(values):
    return values.reshape(values.shape[:-1] + (values.shape[-1] // HD, HD))


def merge_heads(values):
    return values.reshape(values.shape[:-2] + (values.shape[-2] * values.shape[-1],))


def project(operand, weight):
    return lax.dot_general(
        operand, weight, (((operand.ndim - 1,), (0,)), ((), ())), preferred_element_type=jnp.float32
    )


def project_back(operand, weight):
    return lax.dot_general(
        operand, weight, (((operand.ndim - 1,), (1,)), ((), ())), preferred_element_type=jnp.float32
    )


def weight_gradient(operand, gradient):
    flat_operand = operand.reshape(-1, operand.shape[-1])
    flat_gradient = gradient.reshape(-1, gradient.shape[-1])
    return lax.dot_general(
        flat_operand, flat_gradient, (((0,), (0,)), ((), ())), preferred_element_type=jnp.float32
    )


def token_total(gradient):
    return jnp.sum(gradient.astype(jnp.float32).reshape(-1, gradient.shape[-1]), axis=0)


def model_gather(values):
    return lax.all_gather(values, MP, axis=0, tiled=True)


def model_sum(operand_pairs, backward):
    running_total = None
    for operand, weight in operand_pairs:
        if backward:
            product = project_back(operand, weight)
        else:
            product = project(operand, weight)
        running_total = product if running_total is None else running_total + product
    return lax.psum_scatter(
        running_total.astype(jnp.bfloat16), MP, scatter_dimension=0, tiled=True
    ).astype(jnp.float32)


def to_columns(values):
    return lax.all_to_all(
        values.astype(jnp.bfloat16), SEQ, split_axis=0, concat_axis=1, tiled=True
    ).astype(values.dtype)


def to_rows(values):
    return lax.all_to_all(
        values.astype(jnp.bfloat16), SEQ, split_axis=1, concat_axis=0, tiled=True
    ).astype(values.dtype)


def to_query_share(values):
    return lax.all_to_all(values, SEQ, split_axis=0, concat_axis=1, tiled=True)


def masked_softmax(logits, valid_cols, score_scale):
    scores = jnp.where((valid_cols > 0)[None, None, :], logits * score_scale, -1e30)
    highest = jnp.max(scores, axis=-1, keepdims=True)
    powers = jnp.exp(scores - highest)
    return powers / jnp.sum(powers, axis=-1, keepdims=True)


def tied_scale(key_rows):
    return 1.0 / math.sqrt(HD * key_rows.shape[1] * lax.axis_size(SEQ))


def tied_forward(queries, key_rows, value_rows, valid_cols):
    score_scale = tied_scale(key_rows)
    value_all = None
    key_all, value_all = (
        lax.all_gather(key_rows, SEQ, axis=1, tiled=True),
        lax.all_gather(value_rows, SEQ, axis=1, tiled=True),
    )
    query_share = to_query_share(queries)
    logits = jnp.einsum(
        "irhd,jrhd->hij",
        split_heads(query_share),
        split_heads(key_all),
        preferred_element_type=jnp.float32,
    )
    attention = masked_softmax(logits, valid_cols, score_scale)
    attention_all = lax.all_gather(attention.astype(jnp.bfloat16), SEQ, axis=1, tiled=True)
    head_values = jnp.einsum(
        "hij,jrhd->irhd", attention_all, split_heads(value_rows), preferred_element_type=jnp.float32
    )
    return (merge_heads(head_values).astype(jnp.bfloat16), attention, attention_all, value_all)


def tied_backward(grad_heads, queries, key_rows, attention, attention_all, value_all):
    score_scale = tied_scale(key_rows)
    grad_share = to_query_share(grad_heads)
    grad_weights = jnp.einsum(
        "irhd,jrhd->hij",
        split_heads(grad_share),
        split_heads(value_all),
        preferred_element_type=jnp.float32,
    )
    inner_sum = jnp.sum(attention * grad_weights, axis=-1, keepdims=True)
    grad_logits = (attention * (grad_weights - inner_sum)).astype(jnp.bfloat16)
    logits_all = lax.all_gather(grad_logits, SEQ, axis=1, tiled=True)
    grad_query = (
        jnp.einsum(
            "hij,jrhd->irhd", logits_all, split_heads(key_rows), preferred_element_type=jnp.float32
        )
        * score_scale
    )
    grad_key = (
        jnp.einsum(
            "hij,irhd->jrhd", logits_all, split_heads(queries), preferred_element_type=jnp.float32
        )
        * score_scale
    )
    grad_value = jnp.einsum(
        "hij,irhd->jrhd", attention_all, split_heads(grad_heads), preferred_element_type=jnp.float32
    )
    return (
        merge_heads(grad_query).astype(jnp.bfloat16),
        merge_heads(grad_key).astype(jnp.bfloat16),
        merge_heads(grad_value).astype(jnp.bfloat16),
    )


def column_forward(queries, key_rows, value_rows):
    score_scale = 1.0 / math.sqrt(HD)
    scores = (
        jnp.einsum(
            "crhd,cshd->chrs",
            split_heads(queries),
            split_heads(key_rows),
            preferred_element_type=jnp.float32,
        )
        * score_scale
    )
    highest = jnp.max(scores, axis=-1, keepdims=True)
    powers = jnp.exp(scores - highest)
    attention = powers / jnp.sum(powers, axis=-1, keepdims=True)
    attention_low = attention.astype(jnp.bfloat16)
    head_values = jnp.einsum(
        "chrs,cshd->crhd",
        attention_low,
        split_heads(value_rows),
        preferred_element_type=jnp.float32,
    )
    return (merge_heads(head_values).astype(jnp.bfloat16), attention, attention_low)


def column_backward(grad_heads, queries, key_rows, value_rows, attention, attention_low):
    score_scale = 1.0 / math.sqrt(HD)
    grad_split = split_heads(grad_heads)
    grad_weights = jnp.einsum(
        "crhd,cshd->chrs", grad_split, split_heads(value_rows), preferred_element_type=jnp.float32
    )
    grad_value = jnp.einsum(
        "chrs,crhd->cshd", attention_low, grad_split, preferred_element_type=jnp.float32
    )
    inner_sum = jnp.sum(attention * grad_weights, axis=-1, keepdims=True)
    grad_logits = (attention * (grad_weights - inner_sum)).astype(jnp.bfloat16)
    grad_query = (
        jnp.einsum(
            "chrs,cshd->crhd",
            grad_logits,
            split_heads(key_rows),
            preferred_element_type=jnp.float32,
        )
        * score_scale
    )
    grad_key = (
        jnp.einsum(
            "chrs,crhd->cshd", grad_logits, split_heads(queries), preferred_element_type=jnp.float32
        )
        * score_scale
    )
    return (
        merge_heads(grad_query).astype(jnp.bfloat16),
        merge_heads(grad_key).astype(jnp.bfloat16),
        merge_heads(grad_value).astype(jnp.bfloat16),
    )


def norm_backward(values, norm_gain, norm_shift, gradient):
    norm_value, norm_pull = jax.vjp(normalize, values, norm_gain, norm_shift)
    return norm_pull(gradient)


def on_device(
    acts,
    cotangent,
    col_mask,
    ln_row_gain,
    ln_row_bias,
    row_wq,
    row_wk,
    row_wv,
    row_bq,
    row_bv,
    row_wo,
    row_bo,
    ln_col_gain,
    ln_col_bias,
    col_wq,
    col_wk,
    col_wv,
    col_bq,
    col_bv,
    col_wo,
    col_bo,
    ln_ffn_gain,
    ln_ffn_bias,
    ffn_w1,
    ffn_b1,
    ffn_w2,
    ffn_b2,
):
    stream = acts[0].astype(jnp.float32)
    valid_cols = col_mask[0]
    rec_row_in = stream
    normed = normalize(stream, ln_row_gain[0], ln_row_bias[0]).astype(
        jnp.bfloat16
    )
    hidden = model_gather(normed)
    queries = (project(hidden, row_wq[0]) + row_bq[0]).astype(jnp.bfloat16)
    key_rows = project(hidden, row_wk[0]).astype(jnp.bfloat16)
    value_rows = (project(hidden, row_wv[0]) + row_bv[0]).astype(jnp.bfloat16)
    head_values, attention, attention_all, value_all = tied_forward(
        queries, key_rows, value_rows, valid_cols
    )
    stream = stream + model_sum(((head_values, row_wo[0]),), False) + row_bo[0]
    rec_row_hidden = hidden
    rec_row_queries = queries
    rec_row_keys = key_rows
    rec_row_values = value_rows
    rec_row_attention = attention
    rec_row_attention_all = attention_all
    rec_row_value_all = value_all
    rec_row_heads = head_values
    column_stream = to_columns(stream)
    rec_col_in = column_stream
    normed = normalize(column_stream, ln_col_gain[0], ln_col_bias[0]).astype(
        jnp.bfloat16
    )
    hidden = model_gather(normed)
    queries = (project(hidden, col_wq[0]) + col_bq[0]).astype(jnp.bfloat16)
    key_rows = project(hidden, col_wk[0]).astype(jnp.bfloat16)
    value_rows = (project(hidden, col_wv[0]) + col_bv[0]).astype(jnp.bfloat16)
    head_values, attention, attention_low = column_forward(queries, key_rows, value_rows)
    column_stream = (
        column_stream
        + model_sum(((head_values, col_wo[0]),), False)
        + col_bo[0]
    )
    rec_col_hidden = hidden
    rec_col_queries = queries
    rec_col_keys = key_rows
    rec_col_values = value_rows
    rec_col_attention = attention
    rec_col_attention_low = attention_low
    rec_col_heads = head_values
    rec_ffn_in = column_stream
    normed = normalize(column_stream, ln_ffn_gain[0], ln_ffn_bias[0]).astype(
        jnp.bfloat16
    )
    hidden = model_gather(normed)
    up_values = project(hidden, ffn_w1[0]) + ffn_b1[0]
    activated = exact_gelu(up_values).astype(jnp.bfloat16)
    column_stream = (
        column_stream + model_sum(((activated, ffn_w2[0]),), False) + ffn_b2[0]
    )
    rec_ffn_hidden = hidden
    rec_ffn_up = up_values
    rec_ffn_act = activated
    stream = to_rows(column_stream)
    gradient = cotangent[0].astype(jnp.float32)
    column_grad = to_columns(gradient)
    grad_low = column_grad.astype(jnp.bfloat16)
    grad_all = model_gather(grad_low)
    g_ffn_w2 = weight_gradient(rec_ffn_act, grad_all)
    g_ffn_b2 = token_total(grad_low)
    grad_act = project_back(grad_all, ffn_w2[0])
    gelu_value, gelu_pull = jax.vjp(exact_gelu, rec_ffn_up)
    grad_up = gelu_pull(grad_act)[0].astype(jnp.bfloat16)
    g_ffn_w1 = weight_gradient(rec_ffn_hidden, grad_up)
    g_ffn_b1 = token_total(grad_up)
    grad_normed = model_sum(((grad_up, ffn_w1[0]),), True)
    grad_input, grad_gain, grad_shift = norm_backward(
        rec_ffn_in, ln_ffn_gain[0], ln_ffn_bias[0], grad_normed
    )
    g_ln_ffn_gain = grad_gain
    g_ln_ffn_bias = grad_shift
    column_grad = column_grad + grad_input
    grad_low = column_grad.astype(jnp.bfloat16)
    grad_all = model_gather(grad_low)
    g_col_wo = weight_gradient(rec_col_heads, grad_all)
    g_col_bo = token_total(grad_low)
    grad_heads = project_back(grad_all, col_wo[0]).astype(jnp.bfloat16)
    grad_query, grad_key, grad_value = column_backward(
        grad_heads,
        rec_col_queries,
        rec_col_keys,
        rec_col_values,
        rec_col_attention,
        rec_col_attention_low,
    )
    g_col_wq = weight_gradient(rec_col_hidden, grad_query)
    g_col_wk = weight_gradient(rec_col_hidden, grad_key)
    g_col_wv = weight_gradient(rec_col_hidden, grad_value)
    g_col_bq = token_total(grad_query)
    g_col_bv = token_total(grad_value)
    grad_normed = model_sum(
        (
            (grad_query, col_wq[0]),
            (grad_key, col_wk[0]),
            (grad_value, col_wv[0]),
        ),
        True,
    )
    grad_input, grad_gain, grad_shift = norm_backward(
        rec_col_in, ln_col_gain[0], ln_col_bias[0], grad_normed
    )
    g_ln_col_gain = grad_gain
    g_ln_col_bias = grad_shift
    column_grad = column_grad + grad_input
    gradient = to_rows(column_grad)
    grad_low = gradient.astype(jnp.bfloat16)
    grad_all = model_gather(grad_low)
    g_row_wo = weight_gradient(rec_row_heads, grad_all)
    g_row_bo = token_total(grad_low)
    grad_heads = project_back(grad_all, row_wo[0]).astype(jnp.bfloat16)
    grad_query, grad_key, grad_value = tied_backward(
        grad_heads,
        rec_row_queries,
        rec_row_keys,
        rec_row_attention,
        rec_row_attention_all,
        rec_row_value_all,
    )
    g_row_wq = weight_gradient(rec_row_hidden, grad_query)
    g_row_wk = weight_gradient(rec_row_hidden, grad_key)
    g_row_wv = weight_gradient(rec_row_hidden, grad_value)
    g_row_bq = token_total(grad_query)
    g_row_bv = token_total(grad_value)
    grad_normed = model_sum(
        (
            (grad_query, row_wq[0]),
            (grad_key, row_wk[0]),
            (grad_value, row_wv[0]),
        ),
        True,
    )
    grad_input, grad_gain, grad_shift = norm_backward(
        rec_row_in, ln_row_gain[0], ln_row_bias[0], grad_normed
    )
    g_ln_row_gain = grad_gain
    g_ln_row_bias = grad_shift
    gradient = gradient + grad_input
    matrix_totals = (
        lax.psum_scatter(
            g_row_wq[None], (DP, SEQ), scatter_dimension=1, tiled=True
        ),
        lax.psum_scatter(
            g_row_wk[None], (DP, SEQ), scatter_dimension=1, tiled=True
        ),
        lax.psum_scatter(
            g_row_wv[None], (DP, SEQ), scatter_dimension=1, tiled=True
        ),
        lax.psum_scatter(
            g_col_wq[None], (DP, SEQ), scatter_dimension=1, tiled=True
        ),
        lax.psum_scatter(
            g_col_wk[None], (DP, SEQ), scatter_dimension=1, tiled=True
        ),
        lax.psum_scatter(
            g_col_wv[None], (DP, SEQ), scatter_dimension=1, tiled=True
        ),
        lax.psum_scatter(
            g_ffn_w1[None], (DP, SEQ), scatter_dimension=1, tiled=True
        ),
    )
    output_totals = in_one_piece(
        (
            g_row_wo[None].astype(jnp.bfloat16),
            g_col_wo[None].astype(jnp.bfloat16),
            g_ffn_w2[None].astype(jnp.bfloat16),
        ),
        (DP, SEQ),
        2,
        1,
    )
    vector_totals = (
        lax.psum_scatter(
            g_ln_row_gain[None],
            (DP, SEQ, MP),
            scatter_dimension=1,
            tiled=True,
        ),
        lax.psum_scatter(
            g_ln_row_bias[None],
            (DP, SEQ, MP),
            scatter_dimension=1,
            tiled=True,
        ),
        lax.psum_scatter(
            g_row_bo[None], (DP, SEQ, MP), scatter_dimension=1, tiled=True
        ),
        lax.psum_scatter(
            g_ln_col_gain[None],
            (DP, SEQ, MP),
            scatter_dimension=1,
            tiled=True,
        ),
        lax.psum_scatter(
            g_ln_col_bias[None],
            (DP, SEQ, MP),
            scatter_dimension=1,
            tiled=True,
        ),
        lax.psum_scatter(
            g_col_bo[None], (DP, SEQ, MP), scatter_dimension=1, tiled=True
        ),
        lax.psum_scatter(
            g_ln_ffn_gain[None],
            (DP, SEQ, MP),
            scatter_dimension=1,
            tiled=True,
        ),
        lax.psum_scatter(
            g_ln_ffn_bias[None],
            (DP, SEQ, MP),
            scatter_dimension=1,
            tiled=True,
        ),
        lax.psum_scatter(
            g_ffn_b2[None], (DP, SEQ, MP), scatter_dimension=1, tiled=True
        ),
    )
    bias_totals = lax.psum(
        (
            g_row_bq[None],
            g_row_bv[None],
            g_col_bq[None],
            g_col_bv[None],
            g_ffn_b1[None],
        ),
        (DP, SEQ),
    )
    return (
        stream[None],
        gradient[None],
        vector_totals[0],
        vector_totals[1],
        matrix_totals[0],
        matrix_totals[1],
        matrix_totals[2],
        bias_totals[0],
        bias_totals[1],
        output_totals[0],
        vector_totals[2],
        vector_totals[3],
        vector_totals[4],
        matrix_totals[3],
        matrix_totals[4],
        matrix_totals[5],
        bias_totals[2],
        bias_totals[3],
        output_totals[1],
        vector_totals[5],
        vector_totals[6],
        vector_totals[7],
        matrix_totals[6],
        bias_totals[4],
        output_totals[2],
        vector_totals[8],
    )


def routed(values, target_of):
    dps, seqs, mps = (lax.axis_size(axis) for axis in AXES)
    pairs = []
    for d in range(dps):
        for s in range(seqs):
            for m in range(mps):
                to_d, to_s, to_m = target_of(d, s, m)
                pairs.append(((d * seqs + s) * mps + m, (to_d * seqs + to_s) * mps + to_m))
    return lax.ppermute(values, AXES, pairs)


def shifted(values, step):
    mps = lax.axis_size(MP)
    return routed(values, lambda d, s, m: (d, s, (m + step) % mps))


def to_sibling(values):
    return routed(values, lambda d, s, m: (d ^ 1, s, m))


def to_x(values):
    return routed(values, lambda d, s, m: (d, s ^ 1, m))


def to_y(values):
    return routed(values, lambda d, s, m: (d ^ 2, s, m))


def together(*values):
    return lax.optimization_barrier(values)


def straight(d, s, m):
    return (d // 2 * 2 + s, d % 2, m)


def crossed(d, s, m):
    return (d // 2 * 2 + 1 - s, d % 2, m)


def crossed_back(d, s, m):
    return (d // 2 * 2 + s, 1 - d % 2, m)


def to_work(arrays, extra):
    half = arrays[0].shape[0] // 2
    x = lax.axis_index(SEQ)

    def halves(which):
        return [lax.dynamic_slice_in_dim(a, which * half, half, axis=0) for a in arrays]

    sent = [jnp.concatenate(halves(x) + [extra]), jnp.concatenate(halves(1 - x))]
    mine, other = routed(sent[0], straight), routed(sent[1], crossed)
    found = [
        jnp.concatenate([mine[i * half : (i + 1) * half], other[i * half : (i + 1) * half]])
        for i in range(len(arrays))
    ]
    return found, mine[len(arrays) * half :], sent


def send_from_work(values):
    half = values.shape[0] // 2
    return routed(values[:half], straight), routed(values[half:], crossed_back)


def from_work(mine, other):
    x = lax.axis_index(SEQ)
    halves = [jnp.where(x == 0, mine, other), jnp.where(x == 0, other, mine)]
    return jnp.concatenate(halves).astype(jnp.float32)[None, :, None]


def dot(a, b, dims):
    return lax.dot_general(a, b, (dims, ((), ())), preferred_element_type=jnp.float32)


def low(values):
    return values.astype(jnp.bfloat16)


def norm_parts(values):
    average = jnp.mean(values, axis=-1, keepdims=True)
    centred = values - average
    scale = lax.rsqrt(jnp.mean(centred * centred, axis=-1, keepdims=True) + EPSILON)
    return centred * scale, scale


def norm_pull(unit, scale, norm_gain, gradient):
    q = gradient * norm_gain
    return (
        q - jnp.mean(q, axis=-1, keepdims=True) - unit * jnp.mean(q * unit, axis=-1, keepdims=True)
    ) * scale


def all_tokens(values):
    return values.reshape(-1, values.shape[-1])


def total(values):
    return jnp.sum(values.astype(jnp.float32).reshape(-1, values.shape[-1]), axis=0)


ANYWHERE = pl.BlockSpec(memory_space=pl.ANY)
IN_VMEM = pl.BlockSpec(memory_space=pltpu.VMEM)
IN_SMEM = pl.BlockSpec(memory_space=pltpu.SMEM)
BIT_Y, BIT_CORE, BIT_X = 4, 2, 1
X_FIRST = (0, BIT_Y, BIT_X, BIT_X | BIT_Y)
Y_FIRST = (0, BIT_X, BIT_Y, BIT_X | BIT_Y)
PAIR = 2 * HD


def kernel_call(body, name, in_memory, outs, scratch, flops, args, scalars=(), waits=()):
    count, given = len(args), body
    if waits:
        args = list(args) + list(waits)
        in_memory = tuple(in_memory) + tuple(range(count, len(args)))

        def body(*refs):
            given(*refs[:count], *refs[len(args) :])

    moved = sum(a.size * a.dtype.itemsize for a in args) + sum(
        math.prod(shape) * jnp.dtype(kind).itemsize for shape, kind in outs
    )
    return pl.pallas_call(
        body,
        name=name,
        out_shape=[jax.ShapeDtypeStruct(shape, kind) for shape, kind in outs],
        in_specs=[
            ANYWHERE if i in in_memory else (IN_SMEM if i in scalars else IN_VMEM)
            for i in range(len(args))
        ],
        out_specs=[IN_VMEM] * len(outs),
        scratch_shapes=scratch,
        cost_estimate=pl.CostEstimate(flops=flops, bytes_accessed=moved, transcendentals=0),
    )(*args)


def mm(a, b):
    return lax.dot_general(a, b, (((1,), (0,)), ((), ())), preferred_element_type=jnp.float32)


def mm_nt(a, b):
    return lax.dot_general(a, b, (((1,), (1,)), ((), ())), preferred_element_type=jnp.float32)


def mm_tn(a, b):
    return lax.dot_general(a, b, (((0,), (0,)), ((), ())), preferred_element_type=jnp.float32)


def turned(values):
    return jnp.transpose(values.astype(jnp.float32)).astype(jnp.bfloat16)


def row_sum(values):
    return jnp.sum(values, axis=0, keepdims=True)


def lanes_below(shape):
    return lax.broadcasted_iota(jnp.int32, shape, 1) < HD


def merged(first, second, slot):
    if slot == 0:
        return jnp.where(lanes_below(first.shape), first, pltpu.roll(second, HD, 1))
    return jnp.where(lanes_below(first.shape), pltpu.roll(first, HD, 1), second)


def joined(pieces, slot):
    pieces = [p.astype(jnp.float32) for p in pieces]
    if len(pieces) % 2:
        pieces = pieces + [jnp.zeros_like(pieces[0])]
    return jnp.concatenate(
        [merged(pieces[i], pieces[i + 1], slot) for i in range(0, len(pieces), 2)], axis=1
    )


def parted(slot0, slot1, piece):
    at = piece // 2 * PAIR
    a, b = slot0[:, at : at + PAIR], slot1[:, at : at + PAIR]
    return merged(a, b, piece % 2)


def load_shards(rank, own, parts, target, sems):
    shards, half = target.shape[0], parts[1].shape[1]
    copies = [pltpu.make_async_copy(own, target.at[0], sems.at[0])]
    for bit, (away, near1, near2, pair1, pair2) in ((0, parts[:5]), (BIT_CORE, parts[5:])):
        found = (
            (0, 0, away.at[:, pl.ds(0, half)]),
            (0, 1, away.at[:, pl.ds(half, half)]),
            (BIT_X, 0, near1),
            (BIT_Y, 1, near2),
            (BIT_Y, 0, pair1.at[0]),
            (BIT_X, 1, pair2.at[0]),
            (BIT_X | BIT_Y, 0, pair1.at[1]),
            (BIT_X | BIT_Y, 1, pair2.at[1]),
        )
        for bits, which, part in found:
            place = pl.multiple_of(((rank[0] ^ (bit | bits)) * 2 + which) * half, half)
            copies.append(
                pltpu.make_async_copy(
                    part,
                    target.at[pl.ds(1, shards - 1), pl.ds(place, half)],
                    sems.at[len(copies)],
                )
            )
    for copy in copies:
        copy.start()
    return copies


def matrix(shards, t, hs):
    return shards[:, t * hs : (t + 1) * hs].reshape(-1, shards.shape[2])


def finish(copies):
    for copy in copies:
        copy.wait()


def head_map(width):
    feature = lax.broadcasted_iota(jnp.int32, (width, 128), 0) // HD
    return (feature == lax.broadcasted_iota(jnp.int32, (width, 128), 1)).astype(jnp.bfloat16)


def head_total(product, ones):
    upper = product.astype(jnp.bfloat16)
    lower = (product - upper.astype(jnp.float32)).astype(jnp.bfloat16)
    return mm(upper, ones) + mm(lower, ones)


def over_features(values, ones):
    return mm_nt(values.astype(jnp.bfloat16), ones)


def pack_kernel(rank, q, k, v, wo, wr, bias, w1, w2, own_out, share_out, ffn_out, sems):
    rows1 = w1.shape[1]
    copies = [
        pltpu.make_async_copy(w1.at[rank[0]], ffn_out.at[pl.ds(0, rows1)], sems.at[0]),
        pltpu.make_async_copy(
            w2.at[rank[0]], ffn_out.at[pl.ds(rows1, w2.shape[1])], sems.at[1]
        ),
    ]
    for copy in copies:
        copy.start()
    hs = wo.shape[0]
    for i, part in enumerate((q, k, v)):
        own_out[i * hs : (i + 1) * hs] = part[...]
    own_out[3 * hs : 4 * hs] = wo[...]
    own_out[4 * hs : 5 * hs] = wr[...]
    rest = own_out.shape[0] - 5 * hs
    own_out[5 * hs :] = jnp.zeros((rest, own_out.shape[1]), jnp.bfloat16)
    rows = own_out.shape[0] // 8
    share_out[:rows] = own_out[pl.ds(pl.multiple_of(rank[0] * rows, rows), rows)]
    share_out[rows:] = bias[...]
    finish(copies)


def row_project_kernel(blocks, half, heads, *refs):
    hidden, (w, b, q_out, kv_out) = refs[:blocks], refs[blocks:]
    for k in range(blocks):
        y = (mm_nt(hidden[k][...], w[...]) + b[...]).astype(jnp.bfloat16).astype(jnp.float32)
        for p in range(3 * heads):
            piece = parted(y[:half], y[half:], p).astype(jnp.bfloat16)
            if p < heads:
                q_out[p, k * half : (k + 1) * half] = piece
            else:
                kv_out[p - heads, k * half : (k + 1) * half] = piece


def row_attend_kernel(heads, half, scale, q, kv, kv_sibling, mask, p_out, *o_out):
    blocks = len(o_out)

    def one_head(h, carry):
        keys = [kv[h], pltpu.roll(kv_sibling[h].astype(jnp.float32), HD, 1).astype(jnp.bfloat16)]
        values = [
            kv[heads + h],
            pltpu.roll(kv_sibling[heads + h].astype(jnp.float32), HD, 1).astype(jnp.bfloat16),
        ]
        keys, values = jnp.concatenate(keys, axis=0), jnp.concatenate(values, axis=0)
        for k in range(blocks):
            rows = slice(k * half, (k + 1) * half)
            scores = jnp.where(mask[...] > 0, mm_nt(q[h, rows], keys) * scale, -1e30)
            powers = jnp.exp(scores - jnp.max(scores, axis=-1, keepdims=True))
            weights = (powers / jnp.sum(powers, axis=-1, keepdims=True)).astype(jnp.bfloat16)
            p_out[h, rows] = weights
            o_out[k][h] = mm(weights, values).astype(jnp.bfloat16)
        return carry

    lax.fori_loop(0, heads, one_head, 0)


def row_attend_back_kernel(
    heads, half, blocks, scale, q, kv, kv_sibling, p, *refs
):
    d, (q_out, kv_out, sibling_out) = refs[:blocks], refs[blocks:]
    keys_here = kv.shape[1]

    def one_head(h, carry):
        keys = [kv[h], pltpu.roll(kv_sibling[h].astype(jnp.float32), HD, 1).astype(jnp.bfloat16)]
        values = [
            kv[heads + h],
            pltpu.roll(kv_sibling[heads + h].astype(jnp.float32), HD, 1).astype(jnp.bfloat16),
        ]
        keys, values = jnp.concatenate(keys, axis=0), jnp.concatenate(values, axis=0)
        grad_o = jnp.concatenate([d[k][h] for k in range(blocks)], axis=0)
        weights = p[h]
        weights32 = weights.astype(jnp.float32)
        grad_weights = mm_nt(grad_o, values)
        inner = jnp.sum(weights32 * grad_weights, axis=-1, keepdims=True)
        grad_logits = (weights32 * (grad_weights - inner)).astype(jnp.bfloat16)
        q_out[h] = (mm(grad_logits, keys) * scale).astype(jnp.bfloat16)
        grad_k = mm_tn(grad_logits, q[h]) * scale
        grad_v = mm_tn(weights, grad_o)
        kv_out[h], kv_out[heads + h] = grad_k[:keys_here], grad_v[:keys_here]
        sibling_out[h] = pltpu.roll(grad_k[keys_here:], HD, 1).astype(jnp.bfloat16)
        sibling_out[heads + h] = pltpu.roll(grad_v[keys_here:], HD, 1).astype(jnp.bfloat16)
        return carry

    lax.fori_loop(0, heads, one_head, 0)


def row_project_back_kernel(blocks, half, heads, rank, *refs):
    hidden = refs[:blocks]
    w, gain, bias, gq, gkv, gkv_sibling, col_sums, ffn_sums, b1_sums = refs[blocks : blocks + 9]
    keep_out, theirs_out, bias_out = refs[blocks + 9 : blocks + 12]
    send_out, (sums, g, whole) = refs[blocks + 12 : 2 * blocks + 12], refs[2 * blocks + 12 :]
    sums[...] = jnp.zeros_like(sums)
    sums[2:3] = col_sums[3:4]
    sums[3:6] = col_sums[0:3]
    sums[6:9] = ffn_sums[0:3]
    sums[9:11] = col_sums[4:6]
    for k in range(blocks):
        rows = slice(k * half, (k + 1) * half)
        pieces = [gq[h, rows].astype(jnp.float32) for h in range(heads)] + [
            (gkv[i, rows] + gkv_sibling[i, rows].astype(jnp.float32))
            .astype(jnp.bfloat16)
            .astype(jnp.float32)
            for i in range(2 * heads)
        ]
        y = jnp.concatenate([joined(pieces, 0), joined(pieces, 1)], axis=0).astype(jnp.bfloat16)
        g[2 * k * half : 2 * (k + 1) * half] = y
        grad = mm(y, w[...])
        send_out[k][: 2 * half] = grad.astype(jnp.bfloat16)
        unit = (hidden[k][...].astype(jnp.float32) - bias[...]) / gain[...]
        sums[0:1] += row_sum(grad * unit)
        sums[1:2] += row_sum(grad)
    for k in range(blocks):
        sums[11:12] = b1_sums[k : k + 1]
        send_out[k][2 * half :] = sums[...].astype(jnp.bfloat16)
    bias_out[...] = row_sum(g[...].astype(jnp.float32))
    weight = mm_tn(hidden[0][...], g[: 2 * half])
    for k in range(1, blocks):
        weight += mm_tn(hidden[k][...], g[2 * k * half : 2 * (k + 1) * half])
    whole[...] = weight
    rows = keep_out.shape[0] // 4
    for i, bits in enumerate(X_FIRST):
        here = slice(i * rows, (i + 1) * rows)
        for peer, target in ((bits, keep_out), (bits | BIT_CORE, theirs_out)):
            at = pl.multiple_of((rank[0] ^ peer) * rows, rows)
            target[here] = whole[pl.ds(at, rows)].astype(jnp.bfloat16)


def norm_in_kernel(values, gain, bias):
    unit, scale = norm_parts(values)
    return unit, scale, (unit * gain + bias).astype(jnp.bfloat16)


def column_kernel(
    blocks, heads, rank, stream, own, row_bo, gain, bias, bq, bv, col_bo, ffn_gain, ffn_bias,
    *refs
):
    o, parts, refs = refs[:blocks], refs[blocks : blocks + 10], refs[blocks + 10 :]
    row_heads_out, row_out, normed_out, q_out, k_out, v_out, heads_out, col_out, ffn_out = refs[:9]
    shards, sems = refs[9:]
    hs = heads * HD
    half = stream.shape[0] // 2
    copies = load_shards(rank, own, parts, shards, sems)
    pieces = [o[-k % blocks][h] for k in range(blocks) for h in range(heads)]
    row_heads = jnp.concatenate([joined(pieces, 0), joined(pieces, 1)], axis=0).astype(
        jnp.bfloat16
    )
    row_heads_out[...] = row_heads
    finish(copies)
    after_row = stream[...] + mm(row_heads, matrix(shards, 4, hs)) + row_bo[...]
    row_out[...] = after_row
    _, _, normed = norm_in_kernel(after_row, gain[...], bias[...])
    normed_out[...] = normed
    q = (mm_nt(normed, matrix(shards, 0, hs)) + bq[...]).astype(jnp.bfloat16)
    q_out[...] = q
    k = mm_nt(normed, matrix(shards, 1, hs)).astype(jnp.bfloat16)
    k_out[...] = k
    v = (mm_nt(normed, matrix(shards, 2, hs)) + bv[...]).astype(jnp.bfloat16)
    v_out[...] = v
    ones = head_map(stream.shape[1])
    k32, v32 = k.astype(jnp.float32), v.astype(jnp.float32)
    k_gap = k32[:half] - k32[half:]
    for r in range(2):
        rows = slice(r * half, (r + 1) * half)
        gap = head_total(q[rows].astype(jnp.float32) * k_gap, ones) * (1.0 / math.sqrt(HD))
        first = over_features(1.0 / (1.0 + jnp.exp(-gap)), ones)
        second = over_features(1.0 / (1.0 + jnp.exp(gap)), ones)
        heads_out[rows] = (first * v32[:half] + second * v32[half:]).astype(jnp.bfloat16)
    after_col = after_row + mm(heads_out[...], matrix(shards, 3, hs)) + col_bo[...]
    col_out[...] = after_col
    _, _, ffn_normed = norm_in_kernel(after_col, ffn_gain[...], ffn_bias[...])
    ffn_out[...] = ffn_normed


def ffn_kernel(
    rank, normed, stream, grad_low, gathered, b1, b2, gain,
    out, grad_out, low_out, weights_out, sums_out, b1_out,
    w1, w2, normed_t, low_t, total_out, total_back, sems,
):
    blocks, peers, rows1, size = w1.shape
    width = normed.shape[1]
    copies = []
    for k in range(blocks):
        shard = (rank[1] + blocks - k) % blocks
        pair = (
            (gathered.at[:, shard, pl.ds(0, rows1)], w1.at[k]),
            (gathered.at[:, shard, pl.ds(rows1, w2.shape[2])], w2.at[k]),
        )
        for i, (source, target) in enumerate(pair):
            copies.append(pltpu.make_async_copy(source, target, sems.at[2 * k + i]))
            copies[-1].start()
    normed_t[...] = turned(normed[...])
    low_t[...] = turned(grad_low[...])
    total_out[...] = jnp.zeros_like(total_out)
    total_back[...] = jnp.zeros_like(total_back)
    finish(copies)

    def one_shard(k, carry):
        shard = (rank[1] + blocks - k) % blocks
        weight1 = w1[k].reshape(width, size)
        weight2 = w2[k].reshape(size, width)
        up = mm(normed[...], weight1) + b1[pl.ds(k, 1)]
        below = 0.5 * (1.0 + lax.erf(up * (1.0 / math.sqrt(2.0))))
        density = jnp.exp(up * up * -0.5) * (1.0 / math.sqrt(2.0 * math.pi))
        activated = (up * below).astype(jnp.bfloat16)
        grad_up = (mm_nt(grad_low[...], weight2) * (below + up * density)).astype(jnp.bfloat16)
        total_out[...] += mm(activated, weight2)
        total_back[...] += mm_nt(grad_up, weight1)
        b1_out[pl.ds(k, 1)] = row_sum(grad_up.astype(jnp.float32))
        for i, (left, right) in enumerate(((normed_t, grad_up), (low_t, activated))):
            product = mm(left[...], right).astype(jnp.bfloat16).reshape(peers, rows1, size)
            weights_out[:, shard, :, i * size : (i + 1) * size] = product
        return carry

    lax.fori_loop(0, blocks, one_shard, 0)
    out[...] = (stream[...] + total_out[...] + b2[...]).astype(jnp.bfloat16)
    unit, scale = norm_parts(stream[...])
    grad_normed = total_back[...]
    sums_out[...] = jnp.zeros_like(sums_out)
    sums_out[0:1] = row_sum(grad_normed * unit)
    sums_out[1:2] = row_sum(grad_normed)
    sums_out[2:3] = row_sum(grad_low[...].astype(jnp.float32))
    grad = grad_low[...].astype(jnp.float32) + norm_pull(unit, scale, gain[...], grad_normed)
    grad_out[...] = grad
    low_out[...] = grad.astype(jnp.bfloat16)


def column_back_kernel(
    blocks, heads, rank, grad, grad_low, q, k, v, row_stream, own, gain, *refs
):
    parts, refs = refs[:10], refs[10:]
    gq_out, gk_out, gv_out, grad_out, low_out, sums_out = refs[:6]
    d_out, (shards, sems) = refs[6 : 6 + blocks], refs[6 + blocks :]
    hs, width = heads * HD, grad.shape[1]
    half = grad.shape[0] // 2
    copies = load_shards(rank, own, parts, shards, sems)
    ones = head_map(width)
    finish(copies)
    grad_heads = mm_nt(grad_low[...], matrix(shards, 3, hs)).astype(jnp.bfloat16)
    g32 = grad_heads.astype(jnp.float32)
    k32, v32, q32 = (a[...].astype(jnp.float32) for a in (k, v, q))
    k_gap, v_gap = k32[:half] - k32[half:], v32[:half] - v32[half:]
    factor = 1.0 / math.sqrt(HD)
    grad_k, grad_v = 0.0, [0.0, 0.0]
    for r in range(2):
        rows = slice(r * half, (r + 1) * half)
        gap = head_total(q32[rows] * k_gap, ones) * factor
        first, second = 1.0 / (1.0 + jnp.exp(-gap)), 1.0 / (1.0 + jnp.exp(gap))
        pull = head_total(g32[rows] * v_gap, ones)
        grad_logit = over_features(first * second * pull, ones)
        gq_out[rows] = (grad_logit * k_gap * factor).astype(jnp.bfloat16)
        grad_k += grad_logit * q32[rows] * factor
        for s, weight in enumerate((first, second)):
            grad_v[s] += over_features(weight, ones) * g32[rows]
    gk_out[:half] = grad_k.astype(jnp.bfloat16)
    gk_out[half:] = (-grad_k).astype(jnp.bfloat16)
    gv_out[:half] = grad_v[0].astype(jnp.bfloat16)
    gv_out[half:] = grad_v[1].astype(jnp.bfloat16)
    grad_normed = (
        mm(gq_out[...], matrix(shards, 0, hs))
        + mm(gk_out[...], matrix(shards, 1, hs))
        + mm(gv_out[...], matrix(shards, 2, hs))
    )
    unit, scale = norm_parts(row_stream[...])
    total = grad[...] + norm_pull(unit, scale, gain[...], grad_normed)
    grad_out[...] = total
    low = total.astype(jnp.bfloat16)
    low_out[...] = low
    sums_out[...] = jnp.zeros_like(sums_out)
    sums_out[0:1] = row_sum(grad_normed * unit)
    sums_out[1:2] = row_sum(grad_normed)
    sums_out[2:3] = row_sum(grad_low[...].astype(jnp.float32))
    sums_out[3:4] = row_sum(low.astype(jnp.float32))
    sums_out[4:5] = row_sum(gq_out[...].astype(jnp.float32))
    sums_out[5:6] = row_sum(gv_out[...].astype(jnp.float32))
    grad_o = mm_nt(low, matrix(shards, 4, hs)).astype(jnp.bfloat16).astype(jnp.float32)
    for b in range(blocks):
        for h in range(heads):
            piece = parted(grad_o[:half], grad_o[half:], b * heads + h)
            d_out[b][h] = piece.astype(jnp.bfloat16)


def weights_kernel(
    rank, normed, col_low, row_low, gq, gk, gv, col_heads, row_heads, keep_out, send_out, left
):
    width = normed.shape[1]
    rows, kept, part = width // 8, width // 2, width // 2
    for i, source in enumerate((normed, col_low, row_low)):
        left[3 * i] = turned(source[...])
        for order, bits in enumerate((X_FIRST, Y_FIRST)):
            for j in range(8):
                peer = rank[0] ^ (bits[j % 4] | (BIT_CORE if j >= 4 else 0))
                block = left[3 * i, pl.ds(pl.multiple_of(peer * rows, rows), rows)]
                left[3 * i + 1 + order, j * rows : (j + 1) * rows] = block
    for t, right in enumerate((gq, gk, gv, col_heads, row_heads)):
        for order in range(2):
            product = mm(
                left[3 * max(t - 2, 0) + 1 + order], right[:, order * part : (order + 1) * part]
            ).astype(jnp.bfloat16)
            keep_out[order, :, t * part : (t + 1) * part] = product[:kept]
            send_out[order, :, t * part : (t + 1) * part] = product[kept:]


def on_device_columns(
    acts,
    cotangent,
    col_mask,
    ln_row_gain,
    ln_row_bias,
    row_wq,
    row_wk,
    row_wv,
    row_bq,
    row_bv,
    row_wo,
    row_bo,
    ln_col_gain,
    ln_col_bias,
    col_wq,
    col_wk,
    col_wv,
    col_bq,
    col_bv,
    col_wo,
    col_bo,
    ln_ffn_gain,
    ln_ffn_bias,
    ffn_w1,
    ffn_b1,
    ffn_w2,
    ffn_b2,
):
    width = acts.shape[-1]
    hs = row_wq.shape[2]
    heads = hs // HD
    fs = ffn_w1.shape[2]
    ranks = lax.axis_size(DP) * lax.axis_size(SEQ)
    mps = lax.axis_size(MP)
    rank = lax.axis_index(DP) * lax.axis_size(SEQ) + lax.axis_index(SEQ)
    c, z = lax.axis_index(DP) % 2, lax.axis_index(MP)
    f32, b16 = jnp.float32, jnp.bfloat16
    bf_dma = pltpu.SemaphoreType.DMA

    rank_ref = jnp.stack([rank, z]).astype(jnp.int32)

    columns = col_mask.shape[1]
    mask_rows = -(-columns // (8 * width)) * 8
    padded = jnp.pad(col_mask[0].astype(b16), (0, mask_rows * width - columns))
    (start, grad_start), mask, sent = to_work(
        (acts[0, :, 0], cotangent[0, :, 0]), padded.reshape(mask_rows, width)
    )
    mask = mask.reshape(-1)[:columns]
    tokens = start.shape[0]
    half = tokens // 2
    stream = start.astype(f32)
    row_unit, row_scale = norm_parts(stream)
    normed = low(row_unit * ln_row_gain + ln_row_bias)

    def two_parts(v):
        upper = low(v)
        return upper, low(v - upper.astype(f32))

    b1_parts, bq_parts, bv_parts = two_parts(ffn_b1), two_parts(col_bq), two_parts(col_bv)
    bias_rows = jnp.concatenate(
        b1_parts + (jnp.concatenate(bq_parts + bv_parts, axis=1), jnp.zeros((13, width), b16))
    )
    chunk = -(-5 * hs // (32 * ranks)) * 32
    fc, dc = fs // ranks, width // ranks
    own_w1, own_w2 = ffn_w1[0].reshape(ranks, dc, fs), ffn_w2[0].reshape(ranks, fc, width)
    own_attention, pack_attention, pack_ffn = kernel_call(
        pack_kernel,
        "pack",
        (7, 8),
        [((chunk * ranks, width), b16), ((chunk + 16, width), b16), ((dc + fc, width), b16)],
        [bf_dma((2,))],
        0,
        [rank_ref, col_wq[0].T, col_wk[0].T, col_wv[0].T, col_wo[0], row_wo[0], bias_rows]
        + [own_w1, own_w2],
        (0,),
        sent,
    )


    whole_ffn = lax.all_gather(pack_ffn, AXES, axis=0, tiled=False)
    whole_ffn = whole_ffn.reshape(ranks, mps, dc + fc, width)
    pack_attention, normed = together(pack_attention, normed)
    away = [shifted(pack_attention, k) for k in range(1, mps)]
    normed, *away = together(normed, *away)
    away = jnp.stack(away)
    hidden = [shifted(normed, k) for k in range(1, mps)]
    got = together(*hidden, to_x(away[:, : chunk // 2]), to_y(away[:, chunk // 2 : chunk]))
    hidden, near1, near2 = [normed, *got[: mps - 1]], got[mps - 1], got[mps]
    pair1 = to_y(jnp.stack([away[:, : chunk // 2], near1]))
    pair2 = to_x(jnp.stack([away[:, chunk // 2 : chunk], near2]))
    bias_away = away[:, chunk : chunk + 3].astype(f32)
    b1 = jnp.concatenate([ffn_b1, bias_away[:, 0] + bias_away[:, 1]])
    bias_qv = bias_away[:, 2].reshape(mps - 1, 2, 2, hs).sum(axis=2)
    bq = jnp.concatenate([col_bq, bias_qv[:, 0].reshape(1, -1)], axis=1)
    bv = jnp.concatenate([col_bv, bias_qv[:, 1].reshape(1, -1)], axis=1)

    odd = 3 * heads % 2 * HD
    row_w = jnp.concatenate(
        [row_wq[0].T, row_wk[0].T, row_wv[0].T, jnp.zeros((odd, width), b16)]
    )
    row_width = row_w.shape[0]
    row_b = jnp.concatenate(
        [row_bq, jnp.zeros_like(row_bq), row_bv, jnp.zeros((1, odd), f32)], axis=1
    )
    here = mps * half
    q_h, kv_h = kernel_call(
        functools.partial(row_project_kernel, mps, half, heads),
        "row_project",
        (),
        [((heads, here, PAIR), b16), ((2 * heads, here, PAIR), b16)],
        [],
        2 * mps * tokens * width * row_width,
        hidden + [row_w, row_b],
    )
    kv_sibling = to_sibling(kv_h)
    score_scale = 1.0 / math.sqrt(HD * 2)
    near = (z - jnp.arange(mps)) % mps
    pick = (near[:, None] == jnp.arange(mps)).astype(f32)
    mask_blocks = jnp.einsum(
        "kz,zsi->ski", pick, mask.reshape(mps, 2, half).astype(f32), precision="highest"
    )
    mask_near = jnp.where(c == 0, mask_blocks, mask_blocks[::-1]).reshape(1, -1)
    p_h, *o_blocks = kernel_call(
        functools.partial(row_attend_kernel, heads, half, score_scale),
        "row_attend",
        (),
        [((heads, here, 2 * here), b16)] + [((heads, half, PAIR), b16)] * mps,
        [],
        8 * heads * here * here * PAIR,
        [q_h, kv_h, kv_sibling, mask_near],
    )
    o_from = [o_blocks[0]] + [shifted(o_blocks[k], -k) for k in range(1, mps)]
    *o_from, pair1, pair2 = together(*o_from, pair1, pair2)
    parts = [away, near1, near2, pair1, pair2]
    parts += [to_sibling(part) for part in parts]

    weight_scratch = [pltpu.VMEM((mps, chunk * ranks, width), b16), bf_dma((17,))]
    square = tokens * width * width * 2
    row_heads, row_stream, col_normed, col_q, col_k, col_v, col_heads, col_stream, ffn_normed = (
        kernel_call(
            functools.partial(column_kernel, mps, heads),
            "column",
            (2,) + tuple(range(11 + mps, 21 + mps)),
            [
                ((tokens, width), kind)
                for kind in (b16, f32, b16, b16, b16, b16, b16, f32, b16)
            ],
            weight_scratch,
            5 * square,
            [rank_ref, stream, own_attention, row_bo, ln_col_gain, ln_col_bias, bq, bv]
            + [col_bo, ln_ffn_gain, ln_ffn_bias]
            + o_from
            + parts,
            (0,),
        )
    )

    out_low, ffn_grad, col_low, grad_ffn, ffn_sums, grad_b1 = kernel_call(
        ffn_kernel,
        "ffn",
        (4,),
        [
            ((tokens, width), b16),
            ((tokens, width), f32),
            ((tokens, width), b16),
            ((ranks, mps, dc, 2 * fs), b16),
            ((8, width), f32),
            ((mps, fs), f32),
        ],
        [
            pltpu.VMEM((mps, ranks, dc, fs), b16),
            pltpu.VMEM((mps, ranks, fc, width), b16),
            pltpu.VMEM((width, tokens), b16),
            pltpu.VMEM((width, tokens), b16),
            pltpu.VMEM((tokens, width), f32),
            pltpu.VMEM((tokens, width), f32),
            bf_dma((2 * mps,)),
        ],
        12 * tokens * width * fs * mps,
        [rank_ref, ffn_normed, col_stream, grad_start, whole_ffn, b1, ffn_b2, ln_ffn_gain],
        (0,),
    )
    out_halves = send_from_work(out_low)

    grad_q, grad_k, grad_v, row_grad, row_low, col_sums, *d_blocks = kernel_call(
        functools.partial(column_back_kernel, mps, heads),
        "column_back",
        (7,) + tuple(range(9, 19)),
        [
            ((tokens, width), b16),
            ((tokens, width), b16),
            ((tokens, width), b16),
            ((tokens, width), f32),
            ((tokens, width), b16),
            ((8, width), f32),
        ]
        + [((heads, half, PAIR), b16)] * mps,
        weight_scratch,
        5 * square,
        [rank_ref, ffn_grad, col_low, col_q, col_k, col_v, row_stream, own_attention, ln_col_gain]
        + parts,
        (0,),
    )
    d_from = [d_blocks[0]] + [shifted(d_blocks[k], -k) for k in range(1, mps)]
    def both(a, b, here):
        return a[here].astype(f32) + b[here].astype(f32)

    gq_h, gkv_h, gkv_theirs = kernel_call(
        functools.partial(row_attend_back_kernel, heads, half, mps, score_scale),
        "row_attend_back",
        (),
        [
            ((heads, here, PAIR), b16),
            ((2 * heads, here, PAIR), f32),
            ((2 * heads, here, PAIR), b16),
        ],
        [],
        16 * heads * here * here * PAIR,
        [q_h, kv_h, kv_sibling, p_h] + [d_from[-k % mps] for k in range(mps)],
        waits=out_halves,
    )
    gkv_sibling = to_sibling(gkv_theirs)
    att_keep, att_send = kernel_call(
        weights_kernel,
        "weights",
        (),
        [((2, width // 2, 5 * width // 2), b16)] * 2,
        [pltpu.VMEM((9, width, tokens), b16)],
        5 * square,
        [rank_ref, col_normed, col_low, row_low, grad_q, grad_k, grad_v, col_heads, row_heads],
        (0,),
        [gkv_sibling],
    )
    row_keep, row_theirs, row_bias, *g_send = kernel_call(
        functools.partial(row_project_back_kernel, mps, half, heads),
        "row_project_back",
        (),
        [
            ((width // 2, row_width), b16),
            ((width // 2, row_width), b16),
            ((1, row_width), f32),
        ]
        + [((tokens + 16, width), b16)] * mps,
        [
            pltpu.VMEM((16, width), f32),
            pltpu.VMEM((mps * tokens, row_width), b16),
            pltpu.VMEM((width, row_width), f32),
        ],
        4 * mps * tokens * width * row_width,
        [rank_ref] + hidden + [row_w, ln_row_gain, ln_row_bias, gq_h, gkv_h, gkv_sibling]
        + [col_sums, ffn_sums, grad_b1],
        (0,),
        [att_keep],
    )
    part = width // 4
    upper, lower = slice(0, part // 2), slice(part // 2, part)
    att_theirs = to_sibling(att_send)
    hops = ((to_x, to_y), (to_y, to_x))

    def chip_sum(i, here):
        return both(att_keep[i], att_theirs[i], here)

    far = mps // 2
    near = [k for k in range(1, mps) if k != far]
    g_parts = {0: g_send[0], far: shifted(g_send[far], -far)}
    got = together(
        *(shifted(g_send[k], -k) for k in near),
        *(hops[i][0](low(chip_sum(i, slice(part, None)))) for i in range(2)),
        to_sibling(row_theirs),
    )
    g_parts |= dict(zip(near, got))
    arrived, row_peer = got[len(near) : -1], got[-1]
    g_parts[far], *second = together(
        g_parts[far],
        *(
            hops[i][1](low(chip_sum(i, lower) + arrived[i][lower].astype(f32)))
            for i in range(2)
        ),
    )
    g_parts = [g_parts[k] for k in range(mps)]
    grad_normed = sum(g[:tokens].astype(f32) for g in g_parts)
    gradient = row_grad + norm_pull(row_unit, row_scale, ln_row_gain, grad_normed)

    tails = [g[tokens:].astype(f32) for g in g_parts]
    near_sum = sum(t[:9] for t in tails)
    shard = [
        sum(t[row, k * hs : (k + 1) * hs] for k, t in enumerate(tails))[None] for row in (9, 10)
    ]
    shard += [row_bias[:, :hs], row_bias[:, 2 * hs : 3 * hs]]
    summed = jnp.concatenate(
        [near_sum, jnp.concatenate(shard, axis=1), sum(t[11:12] for t in tails)]
    )

    finals = [
        (
            chip_sum(i, upper) + arrived[i][upper].astype(f32) + second[i].astype(f32)
        ).reshape(part // 2, 5, -1, hs)
        for i in range(2)
    ]

    def shard_of(k):
        return finals[k // (mps // 2)][:, :, k % (mps // 2)]

    ffn_mine = lax.psum_scatter(grad_ffn, (DP, SEQ), scatter_dimension=0, tiled=True)[0]
    ffn_mine, gradient = together(ffn_mine, gradient)
    ffn_total = lax.psum_scatter(ffn_mine, MP, scatter_dimension=0, tiled=True)[0].astype(f32)
    got = together(
        *send_from_work(low(gradient)),
        *(shifted(low(shard_of(k)), -k) for k in range(1, mps)),
        to_x(low(both(row_keep, row_peer, slice(part, None)))),
        to_sibling(summed),
    )
    grad_acts = from_work(*got[:2])
    row_arrived, summed = got[-2], summed + got[-1]
    attention_total = shard_of(0) + sum(g.astype(f32) for g in got[2:-2])

    row_total = (
        both(row_keep, row_peer, upper)
        + row_arrived[upper].astype(f32)
        + to_y(low(both(row_keep, row_peer, lower) + row_arrived[lower].astype(f32))).astype(f32)
    )
    diagonal = routed(summed, lambda d, s, m: (d ^ 2, s ^ 1, m))
    summed = summed + to_x(summed) + (to_y(summed) + diagonal)
    device = rank * mps + z
    vectors = summed[:9].reshape(9, ranks * mps, -1)
    vectors = lax.dynamic_index_in_dim(vectors, device, axis=1, keepdims=False)
    biases = summed[9:10]

    def transposed(v):
        return v.T[None]

    return (
        from_work(*out_halves),
        grad_acts,
        vectors[0][None],
        vectors[1][None],
        row_total[:, :hs][None],
        row_total[:, hs : 2 * hs][None],
        row_total[:, 2 * hs : 3 * hs][None],
        biases[:, 2 * hs : 3 * hs],
        biases[:, 3 * hs : 4 * hs],
        transposed(attention_total[:, 4]),
        vectors[2][None],
        vectors[3][None],
        vectors[4][None],
        attention_total[:, 0][None],
        attention_total[:, 1][None],
        attention_total[:, 2][None],
        biases[:, :hs],
        biases[:, hs : 2 * hs],
        transposed(attention_total[:, 3]),
        vectors[5][None],
        vectors[6][None],
        vectors[7][None],
        ffn_total[:, :fs][None],
        summed[10:11],
        transposed(ffn_total[:, fs:]),
        vectors[8][None],
    )


def solution(mesh):
    placed = (
        P(DP, MP, SEQ, None),
        P(DP, MP, SEQ, None),
        P(DP, None),
        P(),
        P(),
        P(None, None, MP),
        P(None, None, MP),
        P(None, None, MP),
        P(None, MP),
        P(None, MP),
        P(None, MP, None),
        P(),
        P(),
        P(),
        P(None, None, MP),
        P(None, None, MP),
        P(None, None, MP),
        P(None, MP),
        P(None, MP),
        P(None, MP, None),
        P(),
        P(),
        P(),
        P(None, None, MP),
        P(None, MP),
        P(None, MP, None),
        P(),
    )
    in_pairs = tuple(mesh.shape[axis] for axis in AXES) == (4, 2, 4)
    return jax.shard_map(
        on_device_columns if in_pairs else on_device,
        mesh=mesh,
        in_specs=placed,
        out_specs=(
            P(DP, MP, SEQ, None),
            P(DP, MP, SEQ, None),
            P(None, (DP, SEQ, MP)),
            P(None, (DP, SEQ, MP)),
            P(None, (DP, SEQ), MP),
            P(None, (DP, SEQ), MP),
            P(None, (DP, SEQ), MP),
            P(None, MP),
            P(None, MP),
            P(None, MP, (DP, SEQ)),
            P(None, (DP, SEQ, MP)),
            P(None, (DP, SEQ, MP)),
            P(None, (DP, SEQ, MP)),
            P(None, (DP, SEQ), MP),
            P(None, (DP, SEQ), MP),
            P(None, (DP, SEQ), MP),
            P(None, MP),
            P(None, MP),
            P(None, MP, (DP, SEQ)),
            P(None, (DP, SEQ, MP)),
            P(None, (DP, SEQ, MP)),
            P(None, (DP, SEQ, MP)),
            P(None, (DP, SEQ), MP),
            P(None, MP),
            P(None, MP, (DP, SEQ)),
            P(None, (DP, SEQ, MP)),
        ),
        check_vma=False,
    )
```

```python
import functools
import math

import jax
import jax.numpy as jnp
from jax import lax
from jax.experimental import pallas as pl
from jax.experimental.pallas import tpu as pltpu
from jax.sharding import PartitionSpec as P

HD = 64
DP, SEQ, MP = AXES = ("dp", "seq", "mp")


EPSILON = 1e-05


def cut_along(shard, dim, peers):
    before, after = (shard.shape[:dim], shard.shape[dim + 1 :])
    return jnp.moveaxis(shard.reshape(*before, peers, -1, *after), dim, 0)


def sent_and_summed(shard, axis, dim):
    blocks = cut_along(shard, dim, lax.axis_size(axis))
    arrived = lax.all_to_all(blocks, axis, split_axis=0, concat_axis=0, tiled=True)
    return arrived.astype(jnp.float32).sum(axis=0)


def in_one_piece(arrays, axis, dim, along):
    ends, at = ([], 0)
    for a in arrays[:-1]:
        at += a.shape[along]
        ends.append(at)
    both = jnp.concatenate(arrays, axis=along)
    return tuple(jnp.split(sent_and_summed(both, axis, dim), ends, axis=along))


def normalize(values, norm_gain, norm_shift):
    average = jnp.mean(values, axis=-1, keepdims=True)
    centred = values - average
    variance = jnp.mean(centred * centred, axis=-1, keepdims=True)
    return centred * lax.rsqrt(variance + EPSILON) * norm_gain + norm_shift


def exact_gelu(values):
    return jax.nn.gelu(values, approximate=False)


def split_heads(values):
    return values.reshape(values.shape[:-1] + (values.shape[-1] // HD, HD))


def merge_heads(values):
    return values.reshape(values.shape[:-2] + (values.shape[-2] * values.shape[-1],))


def project(operand, weight):
    return lax.dot_general(
        operand, weight, (((operand.ndim - 1,), (0,)), ((), ())), preferred_element_type=jnp.float32
    )


def project_back(operand, weight):
    return lax.dot_general(
        operand, weight, (((operand.ndim - 1,), (1,)), ((), ())), preferred_element_type=jnp.float32
    )


def weight_gradient(operand, gradient):
    flat_operand = operand.reshape(-1, operand.shape[-1])
    flat_gradient = gradient.reshape(-1, gradient.shape[-1])
    return lax.dot_general(
        flat_operand, flat_gradient, (((0,), (0,)), ((), ())), preferred_element_type=jnp.float32
    )


def token_total(gradient):
    return jnp.sum(gradient.astype(jnp.float32).reshape(-1, gradient.shape[-1]), axis=0)


def model_gather(values):
    return lax.all_gather(values, MP, axis=0, tiled=True)


def model_sum(operand_pairs, backward):
    running_total = None
    for operand, weight in operand_pairs:
        if backward:
            product = project_back(operand, weight)
        else:
            product = project(operand, weight)
        running_total = product if running_total is None else running_total + product
    return lax.psum_scatter(
        running_total.astype(jnp.bfloat16), MP, scatter_dimension=0, tiled=True
    ).astype(jnp.float32)


def to_columns(values):
    return lax.all_to_all(
        values.astype(jnp.bfloat16), SEQ, split_axis=0, concat_axis=1, tiled=True
    ).astype(values.dtype)


def to_rows(values):
    return lax.all_to_all(
        values.astype(jnp.bfloat16), SEQ, split_axis=1, concat_axis=0, tiled=True
    ).astype(values.dtype)


def to_query_share(values):
    return lax.all_to_all(values, SEQ, split_axis=0, concat_axis=1, tiled=True)


def masked_softmax(logits, valid_cols, score_scale):
    scores = jnp.where((valid_cols > 0)[None, None, :], logits * score_scale, -1e30)
    highest = jnp.max(scores, axis=-1, keepdims=True)
    powers = jnp.exp(scores - highest)
    return powers / jnp.sum(powers, axis=-1, keepdims=True)


def tied_scale(key_rows):
    return 1.0 / math.sqrt(HD * key_rows.shape[1] * lax.axis_size(SEQ))


def tied_forward(queries, key_rows, value_rows, valid_cols):
    score_scale = tied_scale(key_rows)
    value_all = None
    key_all, value_all = (
        lax.all_gather(key_rows, SEQ, axis=1, tiled=True),
        lax.all_gather(value_rows, SEQ, axis=1, tiled=True),
    )
    query_share = to_query_share(queries)
    logits = jnp.einsum(
        "irhd,jrhd->hij",
        split_heads(query_share),
        split_heads(key_all),
        preferred_element_type=jnp.float32,
    )
    attention = masked_softmax(logits, valid_cols, score_scale)
    attention_all = lax.all_gather(attention.astype(jnp.bfloat16), SEQ, axis=1, tiled=True)
    head_values = jnp.einsum(
        "hij,jrhd->irhd", attention_all, split_heads(value_rows), preferred_element_type=jnp.float32
    )
    return (merge_heads(head_values).astype(jnp.bfloat16), attention, attention_all, value_all)


def tied_backward(grad_heads, queries, key_rows, attention, attention_all, value_all):
    score_scale = tied_scale(key_rows)
    grad_share = to_query_share(grad_heads)
    grad_weights = jnp.einsum(
        "irhd,jrhd->hij",
        split_heads(grad_share),
        split_heads(value_all),
        preferred_element_type=jnp.float32,
    )
    inner_sum = jnp.sum(attention * grad_weights, axis=-1, keepdims=True)
    grad_logits = (attention * (grad_weights - inner_sum)).astype(jnp.bfloat16)
    logits_all = lax.all_gather(grad_logits, SEQ, axis=1, tiled=True)
    grad_query = (
        jnp.einsum(
            "hij,jrhd->irhd", logits_all, split_heads(key_rows), preferred_element_type=jnp.float32
        )
        * score_scale
    )
    grad_key = (
        jnp.einsum(
            "hij,irhd->jrhd", logits_all, split_heads(queries), preferred_element_type=jnp.float32
        )
        * score_scale
    )
    grad_value = jnp.einsum(
        "hij,irhd->jrhd", attention_all, split_heads(grad_heads), preferred_element_type=jnp.float32
    )
    return (
        merge_heads(grad_query).astype(jnp.bfloat16),
        merge_heads(grad_key).astype(jnp.bfloat16),
        merge_heads(grad_value).astype(jnp.bfloat16),
    )


def column_forward(queries, key_rows, value_rows):
    score_scale = 1.0 / math.sqrt(HD)
    scores = (
        jnp.einsum(
            "crhd,cshd->chrs",
            split_heads(queries),
            split_heads(key_rows),
            preferred_element_type=jnp.float32,
        )
        * score_scale
    )
    highest = jnp.max(scores, axis=-1, keepdims=True)
    powers = jnp.exp(scores - highest)
    attention = powers / jnp.sum(powers, axis=-1, keepdims=True)
    attention_low = attention.astype(jnp.bfloat16)
    head_values = jnp.einsum(
        "chrs,cshd->crhd",
        attention_low,
        split_heads(value_rows),
        preferred_element_type=jnp.float32,
    )
    return (merge_heads(head_values).astype(jnp.bfloat16), attention, attention_low)


def column_backward(grad_heads, queries, key_rows, value_rows, attention, attention_low):
    score_scale = 1.0 / math.sqrt(HD)
    grad_split = split_heads(grad_heads)
    grad_weights = jnp.einsum(
        "crhd,cshd->chrs", grad_split, split_heads(value_rows), preferred_element_type=jnp.float32
    )
    grad_value = jnp.einsum(
        "chrs,crhd->cshd", attention_low, grad_split, preferred_element_type=jnp.float32
    )
    inner_sum = jnp.sum(attention * grad_weights, axis=-1, keepdims=True)
    grad_logits = (attention * (grad_weights - inner_sum)).astype(jnp.bfloat16)
    grad_query = (
        jnp.einsum(
            "chrs,cshd->crhd",
            grad_logits,
            split_heads(key_rows),
            preferred_element_type=jnp.float32,
        )
        * score_scale
    )
    grad_key = (
        jnp.einsum(
            "chrs,crhd->cshd", grad_logits, split_heads(queries), preferred_element_type=jnp.float32
        )
        * score_scale
    )
    return (
        merge_heads(grad_query).astype(jnp.bfloat16),
        merge_heads(grad_key).astype(jnp.bfloat16),
        merge_heads(grad_value).astype(jnp.bfloat16),
    )


def norm_backward(values, norm_gain, norm_shift, gradient):
    norm_value, norm_pull = jax.vjp(normalize, values, norm_gain, norm_shift)
    return norm_pull(gradient)


def on_device(
    acts,
    cotangent,
    col_mask,
    ln_row_gain,
    ln_row_bias,
    row_wq,
    row_wk,
    row_wv,
    row_bq,
    row_bv,
    row_wo,
    row_bo,
    ln_col_gain,
    ln_col_bias,
    col_wq,
    col_wk,
    col_wv,
    col_bq,
    col_bv,
    col_wo,
    col_bo,
    ln_ffn_gain,
    ln_ffn_bias,
    ffn_w1,
    ffn_b1,
    ffn_w2,
    ffn_b2,
):
    stream = acts[0].astype(jnp.float32)
    valid_cols = col_mask[0]
    rec_row_in = stream
    normed = normalize(stream, ln_row_gain[0], ln_row_bias[0]).astype(
        jnp.bfloat16
    )
    hidden = model_gather(normed)
    queries = (project(hidden, row_wq[0]) + row_bq[0]).astype(jnp.bfloat16)
    key_rows = project(hidden, row_wk[0]).astype(jnp.bfloat16)
    value_rows = (project(hidden, row_wv[0]) + row_bv[0]).astype(jnp.bfloat16)
    head_values, attention, attention_all, value_all = tied_forward(
        queries, key_rows, value_rows, valid_cols
    )
    stream = stream + model_sum(((head_values, row_wo[0]),), False) + row_bo[0]
    rec_row_hidden = hidden
    rec_row_queries = queries
    rec_row_keys = key_rows
    rec_row_values = value_rows
    rec_row_attention = attention
    rec_row_attention_all = attention_all
    rec_row_value_all = value_all
    rec_row_heads = head_values
    column_stream = to_columns(stream)
    rec_col_in = column_stream
    normed = normalize(column_stream, ln_col_gain[0], ln_col_bias[0]).astype(
        jnp.bfloat16
    )
    hidden = model_gather(normed)
    queries = (project(hidden, col_wq[0]) + col_bq[0]).astype(jnp.bfloat16)
    key_rows = project(hidden, col_wk[0]).astype(jnp.bfloat16)
    value_rows = (project(hidden, col_wv[0]) + col_bv[0]).astype(jnp.bfloat16)
    head_values, attention, attention_low = column_forward(queries, key_rows, value_rows)
    column_stream = (
        column_stream
        + model_sum(((head_values, col_wo[0]),), False)
        + col_bo[0]
    )
    rec_col_hidden = hidden
    rec_col_queries = queries
    rec_col_keys = key_rows
    rec_col_values = value_rows
    rec_col_attention = attention
    rec_col_attention_low = attention_low
    rec_col_heads = head_values
    rec_ffn_in = column_stream
    normed = normalize(column_stream, ln_ffn_gain[0], ln_ffn_bias[0]).astype(
        jnp.bfloat16
    )
    hidden = model_gather(normed)
    up_values = project(hidden, ffn_w1[0]) + ffn_b1[0]
    activated = exact_gelu(up_values).astype(jnp.bfloat16)
    column_stream = (
        column_stream + model_sum(((activated, ffn_w2[0]),), False) + ffn_b2[0]
    )
    rec_ffn_hidden = hidden
    rec_ffn_up = up_values
    rec_ffn_act = activated
    stream = to_rows(column_stream)
    gradient = cotangent[0].astype(jnp.float32)
    column_grad = to_columns(gradient)
    grad_low = column_grad.astype(jnp.bfloat16)
    grad_all = model_gather(grad_low)
    g_ffn_w2 = weight_gradient(rec_ffn_act, grad_all)
    g_ffn_b2 = token_total(grad_low)
    grad_act = project_back(grad_all, ffn_w2[0])
    gelu_value, gelu_pull = jax.vjp(exact_gelu, rec_ffn_up)
    grad_up = gelu_pull(grad_act)[0].astype(jnp.bfloat16)
    g_ffn_w1 = weight_gradient(rec_ffn_hidden, grad_up)
    g_ffn_b1 = token_total(grad_up)
    grad_normed = model_sum(((grad_up, ffn_w1[0]),), True)
    grad_input, grad_gain, grad_shift = norm_backward(
        rec_ffn_in, ln_ffn_gain[0], ln_ffn_bias[0], grad_normed
    )
    g_ln_ffn_gain = grad_gain
    g_ln_ffn_bias = grad_shift
    column_grad = column_grad + grad_input
    grad_low = column_grad.astype(jnp.bfloat16)
    grad_all = model_gather(grad_low)
    g_col_wo = weight_gradient(rec_col_heads, grad_all)
    g_col_bo = token_total(grad_low)
    grad_heads = project_back(grad_all, col_wo[0]).astype(jnp.bfloat16)
    grad_query, grad_key, grad_value = column_backward(
        grad_heads,
        rec_col_queries,
        rec_col_keys,
        rec_col_values,
        rec_col_attention,
        rec_col_attention_low,
    )
    g_col_wq = weight_gradient(rec_col_hidden, grad_query)
    g_col_wk = weight_gradient(rec_col_hidden, grad_key)
    g_col_wv = weight_gradient(rec_col_hidden, grad_value)
    g_col_bq = token_total(grad_query)
    g_col_bv = token_total(grad_value)
    grad_normed = model_sum(
        (
            (grad_query, col_wq[0]),
            (grad_key, col_wk[0]),
            (grad_value, col_wv[0]),
        ),
        True,
    )
    grad_input, grad_gain, grad_shift = norm_backward(
        rec_col_in, ln_col_gain[0], ln_col_bias[0], grad_normed
    )
    g_ln_col_gain = grad_gain
    g_ln_col_bias = grad_shift
    column_grad = column_grad + grad_input
    gradient = to_rows(column_grad)
    grad_low = gradient.astype(jnp.bfloat16)
    grad_all = model_gather(grad_low)
    g_row_wo = weight_gradient(rec_row_heads, grad_all)
    g_row_bo = token_total(grad_low)
    grad_heads = project_back(grad_all, row_wo[0]).astype(jnp.bfloat16)
    grad_query, grad_key, grad_value = tied_backward(
        grad_heads,
        rec_row_queries,
        rec_row_keys,
        rec_row_attention,
        rec_row_attention_all,
        rec_row_value_all,
    )
    g_row_wq = weight_gradient(rec_row_hidden, grad_query)
    g_row_wk = weight_gradient(rec_row_hidden, grad_key)
    g_row_wv = weight_gradient(rec_row_hidden, grad_value)
    g_row_bq = token_total(grad_query)
    g_row_bv = token_total(grad_value)
    grad_normed = model_sum(
        (
            (grad_query, row_wq[0]),
            (grad_key, row_wk[0]),
            (grad_value, row_wv[0]),
        ),
        True,
    )
    grad_input, grad_gain, grad_shift = norm_backward(
        rec_row_in, ln_row_gain[0], ln_row_bias[0], grad_normed
    )
    g_ln_row_gain = grad_gain
    g_ln_row_bias = grad_shift
    gradient = gradient + grad_input
    matrix_totals = (
        lax.psum_scatter(
            g_row_wq[None], (DP, SEQ), scatter_dimension=1, tiled=True
        ),
        lax.psum_scatter(
            g_row_wk[None], (DP, SEQ), scatter_dimension=1, tiled=True
        ),
        lax.psum_scatter(
            g_row_wv[None], (DP, SEQ), scatter_dimension=1, tiled=True
        ),
        lax.psum_scatter(
            g_col_wq[None], (DP, SEQ), scatter_dimension=1, tiled=True
        ),
        lax.psum_scatter(
            g_col_wk[None], (DP, SEQ), scatter_dimension=1, tiled=True
        ),
        lax.psum_scatter(
            g_col_wv[None], (DP, SEQ), scatter_dimension=1, tiled=True
        ),
        lax.psum_scatter(
            g_ffn_w1[None], (DP, SEQ), scatter_dimension=1, tiled=True
        ),
    )
    output_totals = in_one_piece(
        (
            g_row_wo[None].astype(jnp.bfloat16),
            g_col_wo[None].astype(jnp.bfloat16),
            g_ffn_w2[None].astype(jnp.bfloat16),
        ),
        (DP, SEQ),
        2,
        1,
    )
    vector_totals = (
        lax.psum_scatter(
            g_ln_row_gain[None],
            (DP, SEQ, MP),
            scatter_dimension=1,
            tiled=True,
        ),
        lax.psum_scatter(
            g_ln_row_bias[None],
            (DP, SEQ, MP),
            scatter_dimension=1,
            tiled=True,
        ),
        lax.psum_scatter(
            g_row_bo[None], (DP, SEQ, MP), scatter_dimension=1, tiled=True
        ),
        lax.psum_scatter(
            g_ln_col_gain[None],
            (DP, SEQ, MP),
            scatter_dimension=1,
            tiled=True,
        ),
        lax.psum_scatter(
            g_ln_col_bias[None],
            (DP, SEQ, MP),
            scatter_dimension=1,
            tiled=True,
        ),
        lax.psum_scatter(
            g_col_bo[None], (DP, SEQ, MP), scatter_dimension=1, tiled=True
        ),
        lax.psum_scatter(
            g_ln_ffn_gain[None],
            (DP, SEQ, MP),
            scatter_dimension=1,
            tiled=True,
        ),
        lax.psum_scatter(
            g_ln_ffn_bias[None],
            (DP, SEQ, MP),
            scatter_dimension=1,
            tiled=True,
        ),
        lax.psum_scatter(
            g_ffn_b2[None], (DP, SEQ, MP), scatter_dimension=1, tiled=True
        ),
    )
    bias_totals = lax.psum(
        (
            g_row_bq[None],
            g_row_bv[None],
            g_col_bq[None],
            g_col_bv[None],
            g_ffn_b1[None],
        ),
        (DP, SEQ),
    )
    return (
        stream[None],
        gradient[None],
        vector_totals[0],
        vector_totals[1],
        matrix_totals[0],
        matrix_totals[1],
        matrix_totals[2],
        bias_totals[0],
        bias_totals[1],
        output_totals[0],
        vector_totals[2],
        vector_totals[3],
        vector_totals[4],
        matrix_totals[3],
        matrix_totals[4],
        matrix_totals[5],
        bias_totals[2],
        bias_totals[3],
        output_totals[1],
        vector_totals[5],
        vector_totals[6],
        vector_totals[7],
        matrix_totals[6],
        bias_totals[4],
        output_totals[2],
        vector_totals[8],
    )


def routed(values, target_of):
    dps, seqs, mps = (lax.axis_size(axis) for axis in AXES)
    pairs = []
    for d in range(dps):
        for s in range(seqs):
            for m in range(mps):
                to_d, to_s, to_m = target_of(d, s, m)
                pairs.append(((d * seqs + s) * mps + m, (to_d * seqs + to_s) * mps + to_m))
    return lax.ppermute(values, AXES, pairs)


def shifted(values, step):
    mps = lax.axis_size(MP)
    return routed(values, lambda d, s, m: (d, s, (m + step) % mps))


def along_mp(values, pairs):
    groups = range(lax.axis_size(DP) * lax.axis_size(SEQ))
    size = lax.axis_size(MP)
    return lax.ppermute(values, AXES, [(g * size + a, g * size + b) for g in groups for a, b in pairs])


def from_others(values):
    z = lax.axis_index(MP)
    far = along_mp(values, [(0, 2), (1, 3), (2, 0), (3, 1)])
    up = along_mp(values, [(0, 1), (1, 2), (2, 3)])
    down = along_mp(values, [(1, 0), (2, 1), (3, 2)])
    last = along_mp(far, [(2, 3), (1, 0)])
    return [jnp.where(z == 0, last, up), far, jnp.where(z == 3, last, down)]


def to_sibling(values):
    return routed(values, lambda d, s, m: (d ^ 1, s, m))


def to_x(values):
    return routed(values, lambda d, s, m: (d, s ^ 1, m))


def to_y(values):
    return routed(values, lambda d, s, m: (d ^ 2, s, m))


def together(*values):
    return lax.optimization_barrier(values)


def straight(d, s, m):
    return (d // 2 * 2 + s, d % 2, m)


def crossed(d, s, m):
    return (d // 2 * 2 + 1 - s, d % 2, m)


def crossed_back(d, s, m):
    return (d // 2 * 2 + s, 1 - d % 2, m)


def to_work(arrays, extra):
    half = arrays[0].shape[0] // 2
    x = lax.axis_index(SEQ)

    def halves(which):
        return [lax.dynamic_slice_in_dim(a, which * half, half, axis=0) for a in arrays]

    sent = [jnp.concatenate(halves(x) + [extra]), jnp.concatenate(halves(1 - x))]
    mine, other = routed(sent[0], straight), routed(sent[1], crossed)
    found = [
        jnp.concatenate([mine[i * half : (i + 1) * half], other[i * half : (i + 1) * half]])
        for i in range(len(arrays))
    ]
    return found, mine[len(arrays) * half :]


def send_from_work(arrays):
    half = arrays[0].shape[0] // 2
    mine, other = (jnp.concatenate([a[at : at + half] for a in arrays]) for at in (0, half))
    return routed(mine, straight), routed(other, crossed_back)


def dot(a, b, dims):
    return lax.dot_general(a, b, (dims, ((), ())), preferred_element_type=jnp.float32)


def low(values):
    return values.astype(jnp.bfloat16)


def norm_parts(values):
    average = jnp.mean(values, axis=-1, keepdims=True)
    centred = values - average
    scale = lax.rsqrt(jnp.mean(centred * centred, axis=-1, keepdims=True) + EPSILON)
    return centred * scale, scale


def norm_pull(unit, scale, norm_gain, gradient):
    q = gradient * norm_gain
    return (
        q - jnp.mean(q, axis=-1, keepdims=True) - unit * jnp.mean(q * unit, axis=-1, keepdims=True)
    ) * scale


def all_tokens(values):
    return values.reshape(-1, values.shape[-1])


def total(values):
    return jnp.sum(values.astype(jnp.float32).reshape(-1, values.shape[-1]), axis=0)


ANYWHERE = pl.BlockSpec(memory_space=pl.ANY)
IN_VMEM = pl.BlockSpec(memory_space=pltpu.VMEM)
IN_SMEM = pl.BlockSpec(memory_space=pltpu.SMEM)
BIT_Y, BIT_CORE, BIT_X = 4, 2, 1
X_FIRST = (0, BIT_Y, BIT_X, BIT_X | BIT_Y)
Y_FIRST = (0, BIT_X, BIT_Y, BIT_X | BIT_Y)
PAIR = 2 * HD


def kernel_call(body, name, in_memory, outs, scratch, flops, args, scalars=(), waits=(), out_places=()):
    count, given = len(args), body
    if waits:
        args = list(args) + list(waits)
        in_memory = tuple(in_memory) + tuple(range(count, len(args)))

        def body(*refs):
            given(*refs[:count], *refs[len(args) :])

    moved = sum(a.size * a.dtype.itemsize for a in args) + sum(
        math.prod(shape) * jnp.dtype(kind).itemsize for shape, kind in outs
    )
    return pl.pallas_call(
        body,
        name=name,
        out_shape=[jax.ShapeDtypeStruct(shape, kind) for shape, kind in outs],
        in_specs=[
            ANYWHERE if i in in_memory else (IN_SMEM if i in scalars else IN_VMEM)
            for i in range(len(args))
        ],
        out_specs=[ANYWHERE if i in out_places else IN_VMEM for i in range(len(outs))],
        scratch_shapes=scratch,
        cost_estimate=pl.CostEstimate(flops=flops, bytes_accessed=moved, transcendentals=0),
    )(*args)


def mm(a, b):
    return lax.dot_general(a, b, (((1,), (0,)), ((), ())), preferred_element_type=jnp.float32)


def mm_nt(a, b):
    return lax.dot_general(a, b, (((1,), (1,)), ((), ())), preferred_element_type=jnp.float32)


def mm_tn(a, b):
    return lax.dot_general(a, b, (((0,), (0,)), ((), ())), preferred_element_type=jnp.float32)


def turned(values):
    return jnp.transpose(values.astype(jnp.float32)).astype(jnp.bfloat16)


def row_sum(values):
    return jnp.sum(values, axis=0, keepdims=True)


def lanes_below(shape):
    return lax.broadcasted_iota(jnp.int32, shape, 1) < HD


def merged(first, second, slot):
    if slot == 0:
        return jnp.where(lanes_below(first.shape), first, pltpu.roll(second, HD, 1))
    return jnp.where(lanes_below(first.shape), pltpu.roll(first, HD, 1), second)


def joined(pieces, slot):
    pieces = [p.astype(jnp.float32) for p in pieces]
    if len(pieces) % 2:
        pieces = pieces + [jnp.zeros_like(pieces[0])]
    return jnp.concatenate(
        [merged(pieces[i], pieces[i + 1], slot) for i in range(0, len(pieces), 2)], axis=1
    )


def parted(slot0, slot1, piece):
    at = piece // 2 * PAIR
    a, b = slot0[:, at : at + PAIR], slot1[:, at : at + PAIR]
    return merged(a, b, piece % 2)


def loads_of(own, gathered, at, target, sems, first):
    rows, chunk = target.shape[1], own.shape[0] // gathered.shape[0]
    copies = [pltpu.make_async_copy(own.at[pl.ds(at, rows)], target.at[0], sems.at[first])]
    done = 0
    while done < rows:
        place = at + done
        size = min(rows - done, chunk - place % chunk)
        copies.append(
            pltpu.make_async_copy(
                gathered.at[place // chunk, :, pl.ds(place % chunk, size)],
                target.at[pl.ds(1, target.shape[0] - 1), pl.ds(done, size)],
                sems.at[first + len(copies)],
            )
        )
        done += size
    for copy in copies:
        copy.start()
    return copies


def finish(copies):
    for copy in copies:
        copy.wait()


def head_map(width):
    feature = lax.broadcasted_iota(jnp.int32, (width, 128), 0) // HD
    return (feature == lax.broadcasted_iota(jnp.int32, (width, 128), 1)).astype(jnp.bfloat16)


def head_total(product, ones):
    upper = product.astype(jnp.bfloat16)
    lower = (product - upper.astype(jnp.float32)).astype(jnp.bfloat16)
    return mm(upper, ones) + mm(lower, ones)


def over_features(values, ones):
    return mm_nt(values.astype(jnp.bfloat16), ones)


def pack_kernel(
    rank, q, k, v, wo, wr, b1, bq, bv, w1, w2, own_out, share_out, sems
):
    rows, rows1, rows2 = own_out.shape[0] // 8, w1.shape[1], w2.shape[1]
    copies = [
        pltpu.make_async_copy(w1.at[rank[0]], share_out.at[pl.ds(rows, rows1)], sems.at[0]),
        pltpu.make_async_copy(
            w2.at[rank[0]], share_out.at[pl.ds(rows + rows1, rows2)], sems.at[1]
        ),
    ]
    for copy in copies:
        copy.start()
    hs = wo.shape[0]
    for i, part in enumerate((q, k, v, wo, wr)):
        own_out[i * hs : (i + 1) * hs] = part[...]
    at = 5 * hs
    own_out[at:] = jnp.zeros((own_out.shape[0] - at, own_out.shape[1]), jnp.bfloat16)
    place = rows + rows1 + rows2
    share_out[place:] = jnp.zeros((16, own_out.shape[1]), jnp.bfloat16)
    for i, vector in enumerate((b1, bq, bv)):
        upper = vector[...].astype(jnp.bfloat16)
        lower = (vector[...] - upper.astype(jnp.float32)).astype(jnp.bfloat16)
        share_out[place + 2 * i : place + 2 * i + 1, : vector.shape[1]] = upper
        share_out[place + 2 * i + 1 : place + 2 * i + 2, : vector.shape[1]] = lower
    share_out[:rows] = own_out[pl.ds(pl.multiple_of(rank[0] * rows, rows), rows)]
    finish(copies)


def home_kernel(x, mine, other, *outs):
    half = mine.shape[0] // len(outs)
    for i, target in enumerate(outs):
        here = slice(i * half, (i + 1) * half)
        a, b = mine[here].astype(jnp.float32), other[here].astype(jnp.float32)
        target[0, :half, 0] = jnp.where(x[0] == 0, a, b)
        target[0, half:, 0] = jnp.where(x[0] == 0, b, a)


def row_project_kernel(blocks, half, heads, *refs):
    hidden, (w, b, q_out, kv_out) = refs[:blocks], refs[blocks:]
    for k in range(blocks):
        y = (mm_nt(hidden[k][...], w[...]) + b[...]).astype(jnp.bfloat16).astype(jnp.float32)
        for p in range(3 * heads):
            piece = parted(y[:half], y[half:], p).astype(jnp.bfloat16)
            if p < heads:
                q_out[p, k * half : (k + 1) * half] = piece
            else:
                kv_out[p - heads, k * half : (k + 1) * half] = piece


def row_attend_kernel(heads, half, scale, q, kv, kv_sibling, mask, p_out, *o_out):
    blocks = len(o_out)

    def one_head(h, carry):
        keys = [kv[h], pltpu.roll(kv_sibling[h].astype(jnp.float32), HD, 1).astype(jnp.bfloat16)]
        values = [
            kv[heads + h],
            pltpu.roll(kv_sibling[heads + h].astype(jnp.float32), HD, 1).astype(jnp.bfloat16),
        ]
        keys, values = jnp.concatenate(keys, axis=0), jnp.concatenate(values, axis=0)
        for i in range(0, blocks, 2):
            rows = slice(i * half, (i + 2) * half)
            scores = jnp.where(mask[...] > 0, mm_nt(q[h, rows], keys) * scale, -1e30)
            powers = jnp.exp(scores - jnp.max(scores, axis=-1, keepdims=True))
            over = 1.0 / jnp.sum(powers, axis=-1, keepdims=True)
            weights = (powers * over).astype(jnp.bfloat16)
            p_out[h, rows] = weights
            o = mm(weights, values).astype(jnp.bfloat16)
            o_out[i][h], o_out[i + 1][h] = o[:half], o[half:]
        return carry

    lax.fori_loop(0, heads, one_head, 0)


def row_attend_back_kernel(
    heads, half, blocks, scale, q, kv, kv_sibling, p, *refs
):
    d, (q_out, kv_out, sibling_out) = refs[:blocks], refs[blocks:]
    keys_here = kv.shape[1]

    def one_head(h, carry):
        keys = [kv[h], pltpu.roll(kv_sibling[h].astype(jnp.float32), HD, 1).astype(jnp.bfloat16)]
        values = [
            kv[heads + h],
            pltpu.roll(kv_sibling[heads + h].astype(jnp.float32), HD, 1).astype(jnp.bfloat16),
        ]
        keys, values = jnp.concatenate(keys, axis=0), jnp.concatenate(values, axis=0)
        grad_o = jnp.concatenate([d[k][h] for k in range(blocks)], axis=0)
        weights = p[h]
        weights32 = weights.astype(jnp.float32)
        grad_weights = mm_nt(grad_o, values)
        inner = jnp.sum(weights32 * grad_weights, axis=-1, keepdims=True)
        grad_logits = (weights32 * (grad_weights - inner)).astype(jnp.bfloat16)
        q_out[h] = (mm(grad_logits, keys) * scale).astype(jnp.bfloat16)
        grad_k = mm_tn(grad_logits, q[h]) * scale
        grad_v = mm_tn(weights, grad_o)
        kv_out[h], kv_out[heads + h] = grad_k[:keys_here], grad_v[:keys_here]
        sibling_out[h] = pltpu.roll(grad_k[keys_here:], HD, 1).astype(jnp.bfloat16)
        sibling_out[heads + h] = pltpu.roll(grad_v[keys_here:], HD, 1).astype(jnp.bfloat16)
        return carry

    lax.fori_loop(0, heads, one_head, 0)


def row_project_back_kernel(blocks, half, heads, rank, *refs):
    hidden = refs[:blocks]
    w, gain, bias, gq, gkv, gkv_sibling, col_sums, ffn_sums, b1_sums = refs[blocks : blocks + 9]
    keep_out, theirs_out, bias_out = refs[blocks + 9 : blocks + 12]
    send_out, (sums, g, whole) = refs[blocks + 12 : 2 * blocks + 12], refs[2 * blocks + 12 :]
    sums[...] = jnp.zeros_like(sums)
    over_gain = 1.0 / gain[...]
    sums[2:3] = col_sums[3:4]
    sums[3:6] = col_sums[0:3]
    sums[6:9] = ffn_sums[0:3]
    for k in range(blocks):
        rows = slice(k * half, (k + 1) * half)
        pieces = [gq[h, rows].astype(jnp.float32) for h in range(heads)] + [
            (gkv[i, rows] + gkv_sibling[i, rows].astype(jnp.float32))
            .astype(jnp.bfloat16)
            .astype(jnp.float32)
            for i in range(2 * heads)
        ]
        y = jnp.concatenate([joined(pieces, 0), joined(pieces, 1)], axis=0).astype(jnp.bfloat16)
        g[2 * k * half : 2 * (k + 1) * half] = y
        grad = mm(y, w[...])
        send_out[k][: 2 * half] = grad.astype(jnp.bfloat16)
        unit = (hidden[k][...].astype(jnp.float32) - bias[...]) * over_gain
        sums[0:1] += row_sum(grad * unit)
        sums[1:2] += row_sum(grad)
    hs = heads * HD
    for k in range(blocks):
        here = slice(k * hs, (k + 1) * hs)
        sums[9:10, :hs] = col_sums[4:5, here]
        sums[10:11, :hs] = col_sums[5:6, here]
        sums[11:12] = b1_sums[k : k + 1]
        send_out[k][2 * half :] = sums[...].astype(jnp.bfloat16)
    bias_out[...] = row_sum(g[...].astype(jnp.float32))
    weight = mm_tn(hidden[0][...], g[: 2 * half])
    for k in range(1, blocks):
        weight += mm_tn(hidden[k][...], g[2 * k * half : 2 * (k + 1) * half])
    whole[...] = weight
    rows = keep_out.shape[0] // 4
    for i, bits in enumerate(X_FIRST):
        here = slice(i * rows, (i + 1) * rows)
        for peer, target in ((bits, keep_out), (bits | BIT_CORE, theirs_out)):
            at = pl.multiple_of((rank[0] ^ peer) * rows, rows)
            target[here] = whole[pl.ds(at, rows)].astype(jnp.bfloat16)


def norm_in_kernel(values, gain, bias):
    unit, scale = norm_parts(values)
    return unit, scale, (unit * gain + bias).astype(jnp.bfloat16)


def column_kernel(
    blocks, heads, stream, own, gathered, row_bo, gain, bias, bq, bv, col_bo, ffn_gain, ffn_bias,
    *refs
):
    o, refs = refs[:blocks], refs[blocks:]
    row_heads_out, row_out, normed_out, q_out, k_out, v_out, heads_out, col_out, ffn_out = refs[:9]
    wq, wk, wv, wo, wr, sems = refs[9:]
    hs, width = wq.shape[1], stream.shape[1]
    half = stream.shape[0] // 2
    loads, used = [], 0
    for t, target in ((4, wr), (0, wq), (1, wk), (2, wv), (3, wo)):
        loads.append(loads_of(own, gathered, t * hs, target, sems, used))
        used += len(loads[-1])
    pieces = [o[-k % blocks][h] for k in range(blocks) for h in range(heads)]
    row_heads = jnp.concatenate([joined(pieces, 0), joined(pieces, 1)], axis=0).astype(
        jnp.bfloat16
    )
    row_heads_out[...] = row_heads
    finish(loads[0])
    after_row = stream[...] + mm(row_heads, wr[...].reshape(-1, width)) + row_bo[...]
    row_out[...] = after_row
    _, _, normed = norm_in_kernel(after_row, gain[...], bias[...])
    normed_out[...] = normed
    finish(loads[1])
    q = (mm_nt(normed, wq[...].reshape(-1, width)) + bq[...]).astype(jnp.bfloat16)
    q_out[...] = q
    finish(loads[2])
    k = mm_nt(normed, wk[...].reshape(-1, width)).astype(jnp.bfloat16)
    k_out[...] = k
    finish(loads[3])
    v = (mm_nt(normed, wv[...].reshape(-1, width)) + bv[...]).astype(jnp.bfloat16)
    v_out[...] = v
    ones = head_map(width)
    k32, v32 = k.astype(jnp.float32), v.astype(jnp.float32)
    k_gap = k32[:half] - k32[half:]
    for r in range(2):
        rows = slice(r * half, (r + 1) * half)
        gap = head_total(q[rows].astype(jnp.float32) * k_gap, ones) * (1.0 / math.sqrt(HD))
        first = over_features(1.0 / (1.0 + jnp.exp(-gap)), ones)
        second = over_features(1.0 / (1.0 + jnp.exp(gap)), ones)
        heads_out[rows] = (first * v32[:half] + second * v32[half:]).astype(jnp.bfloat16)
    finish(loads[4])
    after_col = after_row + mm(heads_out[...], wo[...].reshape(-1, width)) + col_bo[...]
    col_out[...] = after_col
    _, _, ffn_normed = norm_in_kernel(after_col, ffn_gain[...], ffn_bias[...])
    ffn_out[...] = ffn_normed


def ffn_kernel(
    rank, normed, stream, grad_low, own1, own2, gathered, b1, b2, gain,
    out, grad_out, low_out, weights_out, sums_out, b1_out,
    w1, w2, products, normed_t, low_t, total_out, total_back, sems, out_sems,
):
    blocks, peers, rows1, size = w1.shape
    width = normed.shape[1]
    first = gathered.shape[2] - rows1 - w2.shape[2]
    copies = []
    for k in range(blocks):
        if k == 0:
            pair = [(own1, w1.at[0]), (own2, w2.at[0])]
        else:
            pair = [
                (gathered.at[:, k - 1, pl.ds(first, rows1)], w1.at[k]),
                (gathered.at[:, k - 1, pl.ds(first + rows1, w2.shape[2])], w2.at[k]),
            ]
        for i, (source, target) in enumerate(pair):
            copies.append(pltpu.make_async_copy(source, target, sems.at[2 * k + i]))
            copies[-1].start()
    normed_t[...] = turned(normed[...])
    low_t[...] = turned(grad_low[...])
    total_out[...] = jnp.zeros_like(total_out)
    total_back[...] = jnp.zeros_like(total_back)
    finish(copies[:2])

    def leaving(k):
        shard = (rank[1] + blocks - k) % blocks
        return pltpu.make_async_copy(products.at[k], weights_out.at[:, shard], out_sems.at[k])

    def one_shard(k, carry):
        @pl.when(k > 0)
        def _():
            for i, (at, target) in enumerate(((first, w1), (first + rows1, w2))):
                part = gathered.at[:, k - 1, pl.ds(at, target.shape[2])]
                pltpu.make_async_copy(part, target.at[k], sems.at[2 * k + i]).wait()

        weight1 = w1[k].reshape(width, size)
        weight2 = w2[k].reshape(size, width)
        up = mm(normed[...], weight1) + b1[pl.ds(k, 1)]
        below = 0.5 * (1.0 + lax.erf(up * (1.0 / math.sqrt(2.0))))
        density = jnp.exp(up * up * -0.5) * (1.0 / math.sqrt(2.0 * math.pi))
        activated = (up * below).astype(jnp.bfloat16)
        grad_up = (mm_nt(grad_low[...], weight2) * (below + up * density)).astype(jnp.bfloat16)
        total_out[...] += mm(activated, weight2)
        total_back[...] += mm_nt(grad_up, weight1)
        b1_out[pl.ds(k, 1)] = row_sum(grad_up.astype(jnp.float32))
        for i, (left, right) in enumerate(((normed_t, grad_up), (low_t, activated))):
            product = mm(left[...], right).astype(jnp.bfloat16).reshape(peers, rows1, size)
            products[k, :, :, i * size : (i + 1) * size] = product
        leaving(k).start()
        return carry

    lax.fori_loop(0, blocks, one_shard, 0)
    out[...] = (stream[...] + total_out[...] + b2[...]).astype(jnp.bfloat16)
    unit, scale = norm_parts(stream[...])
    grad_normed = total_back[...]
    sums_out[...] = jnp.zeros_like(sums_out)
    sums_out[0:1] = row_sum(grad_normed * unit)
    sums_out[1:2] = row_sum(grad_normed)
    sums_out[2:3] = row_sum(grad_low[...].astype(jnp.float32))
    grad = grad_low[...].astype(jnp.float32) + norm_pull(unit, scale, gain[...], grad_normed)
    grad_out[...] = grad
    low_out[...] = grad.astype(jnp.bfloat16)
    for k in range(blocks):
        leaving(k).wait()


def column_back_kernel(
    blocks, heads, grad, grad_low, q, k, v, row_stream, own, gathered, gain,
    gq_out, gk_out, gv_out, grad_out, low_out, sums_out, *refs
):
    d_out, (wq, wk, wv, wo, wr, sems) = refs[:blocks], refs[blocks:]
    hs, width = wq.shape[1], grad.shape[1]
    half = grad.shape[0] // 2
    loads, used = [], 0
    for t, target in ((3, wo), (0, wq), (1, wk), (2, wv), (4, wr)):
        loads.append(loads_of(own, gathered, t * hs, target, sems, used))
        used += len(loads[-1])
    ones = head_map(width)
    finish(loads[0])
    grad_heads = mm_nt(grad_low[...], wo[...].reshape(-1, width)).astype(jnp.bfloat16)
    g32 = grad_heads.astype(jnp.float32)
    k32, v32, q32 = (a[...].astype(jnp.float32) for a in (k, v, q))
    k_gap, v_gap = k32[:half] - k32[half:], v32[:half] - v32[half:]
    factor = 1.0 / math.sqrt(HD)
    grad_k, grad_v = 0.0, [0.0, 0.0]
    for r in range(2):
        rows = slice(r * half, (r + 1) * half)
        gap = head_total(q32[rows] * k_gap, ones) * factor
        first, second = 1.0 / (1.0 + jnp.exp(-gap)), 1.0 / (1.0 + jnp.exp(gap))
        pull = head_total(g32[rows] * v_gap, ones)
        grad_logit = over_features(first * second * pull, ones)
        gq_out[rows] = (grad_logit * k_gap * factor).astype(jnp.bfloat16)
        grad_k += grad_logit * q32[rows] * factor
        for s, weight in enumerate((first, second)):
            grad_v[s] += over_features(weight, ones) * g32[rows]
    gk_out[:half] = grad_k.astype(jnp.bfloat16)
    gk_out[half:] = (-grad_k).astype(jnp.bfloat16)
    gv_out[:half] = grad_v[0].astype(jnp.bfloat16)
    gv_out[half:] = grad_v[1].astype(jnp.bfloat16)
    for load in loads[1:4]:
        finish(load)
    grad_normed = (
        mm(gq_out[...], wq[...].reshape(-1, width))
        + mm(gk_out[...], wk[...].reshape(-1, width))
        + mm(gv_out[...], wv[...].reshape(-1, width))
    )
    unit, scale = norm_parts(row_stream[...])
    total = grad[...] + norm_pull(unit, scale, gain[...], grad_normed)
    grad_out[...] = total
    low = total.astype(jnp.bfloat16)
    low_out[...] = low
    sums_out[...] = jnp.zeros_like(sums_out)
    sums_out[0:1] = row_sum(grad_normed * unit)
    sums_out[1:2] = row_sum(grad_normed)
    sums_out[2:3] = row_sum(grad_low[...].astype(jnp.float32))
    sums_out[3:4] = row_sum(low.astype(jnp.float32))
    sums_out[4:5] = row_sum(gq_out[...].astype(jnp.float32))
    sums_out[5:6] = row_sum(gv_out[...].astype(jnp.float32))
    finish(loads[4])
    grad_o = mm_nt(low, wr[...].reshape(-1, width)).astype(jnp.bfloat16).astype(jnp.float32)
    for b in range(blocks):
        for h in range(heads):
            piece = parted(grad_o[:half], grad_o[half:], b * heads + h)
            d_out[b][h] = piece.astype(jnp.bfloat16)


def weights_kernel(
    rank, normed, col_low, row_low, gq, gk, gv, col_heads, row_heads, *refs
):
    keep_outs, send_outs, (left, found, sems) = refs[:2], refs[2:4], refs[4:]
    width = normed.shape[1]
    rows, kept, part = width // 8, width // 2, width // 2
    copies = []
    for i, source in enumerate((normed, col_low, row_low)):
        left[3 * i] = turned(source[...])
        for order, bits in enumerate((X_FIRST, Y_FIRST)):
            for j in range(8):
                peer = rank[0] ^ (bits[j % 4] | (BIT_CORE if j >= 4 else 0))
                block = left[3 * i, pl.ds(pl.multiple_of(peer * rows, rows), rows)]
                left[3 * i + 1 + order, j * rows : (j + 1) * rows] = block
    hs = part // 2
    spare = jnp.zeros((width, found.shape[3] - 5 * hs), jnp.float32)
    for order in range(2):
        products = [
            mm(
                left[3 * max(t - 2, 0) + 1 + order], right[:, order * part : (order + 1) * part]
            )
            for t, right in enumerate((gq, gk, gv, col_heads, row_heads))
        ]
        for k in range(2):
            product = jnp.concatenate(
                [p[:, k * hs : (k + 1) * hs] for p in products] + [spare], axis=1
            ).astype(jnp.bfloat16)
            found[order, k] = product
            for i, target in enumerate((send_outs[order], keep_outs[order])):
                half = found.at[order, k, pl.ds((1 - i) * kept, kept)]
                sem = sems.at[len(copies)]
                copies.append(pltpu.make_async_copy(half, target.at[k], sem))
                copies[-1].start()
    finish(copies)


def on_device_columns(
    acts,
    cotangent,
    col_mask,
    ln_row_gain,
    ln_row_bias,
    row_wq,
    row_wk,
    row_wv,
    row_bq,
    row_bv,
    row_wo,
    row_bo,
    ln_col_gain,
    ln_col_bias,
    col_wq,
    col_wk,
    col_wv,
    col_bq,
    col_bv,
    col_wo,
    col_bo,
    ln_ffn_gain,
    ln_ffn_bias,
    ffn_w1,
    ffn_b1,
    ffn_w2,
    ffn_b2,
):
    width = acts.shape[-1]
    hs = row_wq.shape[2]
    heads = hs // HD
    fs = ffn_w1.shape[2]
    ranks = lax.axis_size(DP) * lax.axis_size(SEQ)
    mps = lax.axis_size(MP)
    rank = lax.axis_index(DP) * lax.axis_size(SEQ) + lax.axis_index(SEQ)
    c, z = lax.axis_index(DP) % 2, lax.axis_index(MP)
    f32, b16 = jnp.float32, jnp.bfloat16
    bf_dma = pltpu.SemaphoreType.DMA

    rank_ref = jnp.stack([rank, z]).astype(jnp.int32)

    columns = col_mask.shape[1]
    mask_rows = -(-columns // (8 * width)) * 8
    padded = jnp.pad(col_mask[0].astype(b16), (0, mask_rows * width - columns))
    (start, grad_start), mask = to_work(
        (acts[0, :, 0], cotangent[0, :, 0]), padded.reshape(mask_rows, width)
    )
    mask = mask.reshape(-1)[:columns]
    tokens = start.shape[0]
    half = tokens // 2
    stream = start.astype(f32)
    row_unit, row_scale = norm_parts(stream)
    normed = low(row_unit * ln_row_gain + ln_row_bias)

    chunk = -(-5 * hs // (16 * ranks)) * 16
    fc, dc = fs // ranks, width // ranks
    own_w1, own_w2 = ffn_w1[0].reshape(ranks, dc, fs), ffn_w2[0].reshape(ranks, fc, width)
    own_attention, pack = kernel_call(
        pack_kernel,
        "pack",
        (9, 10),
        [((chunk * ranks, width), b16), ((chunk + dc + fc + 16, width), b16)],
        [bf_dma((2,))],
        0,
        [rank_ref, col_wq[0].T, col_wk[0].T, col_wv[0].T, col_wo[0], row_wo[0], ffn_b1]
        + [col_bq, col_bv, own_w1, own_w2],
        (0,),
    )


    pack, normed = together(pack, normed)
    away = from_others(pack)
    place = chunk + dc + fc
    whole = lax.all_gather(
        jnp.stack([part[:place] for part in away]), (DP, SEQ), axis=0, tiled=False
    )
    bias_away = jnp.stack([part[place : place + 6] for part in away]).astype(f32)
    bias_away = bias_away.reshape(mps - 1, 3, 2, width).sum(axis=2)
    b1 = jnp.concatenate([ffn_b1, bias_away[:, 0]])
    bq = jnp.concatenate([col_bq, bias_away[:, 1, :hs].reshape(1, -1)], axis=1)
    bv = jnp.concatenate([col_bv, bias_away[:, 2, :hs].reshape(1, -1)], axis=1)

    hidden = [normed] + from_others(normed)
    odd = 3 * heads % 2 * HD
    row_w = jnp.concatenate(
        [row_wq[0].T, row_wk[0].T, row_wv[0].T, jnp.zeros((odd, width), b16)]
    )
    row_width = row_w.shape[0]
    row_b = jnp.concatenate(
        [row_bq, jnp.zeros_like(row_bq), row_bv, jnp.zeros((1, odd), f32)], axis=1
    )
    here = mps * half
    score_scale = 1.0 / math.sqrt(HD * 2)
    near = (z - jnp.arange(mps)) % mps
    pick = (near[:, None] == jnp.arange(mps)).astype(f32)
    mask_blocks = jnp.einsum(
        "kz,zsi->ski", pick, mask.reshape(mps, 2, half).astype(f32), precision="highest"
    )
    mask_near = jnp.where(c == 0, mask_blocks, mask_blocks[::-1]).reshape(1, -1)
    q_h, kv_h = kernel_call(
        functools.partial(row_project_kernel, mps, half, heads),
        "row_project",
        (),
        [((heads, here, PAIR), b16), ((2 * heads, here, PAIR), b16)],
        [],
        2 * mps * tokens * width * row_width,
        hidden + [row_w, row_b],
        waits=[mask_near, grad_start, stream, b1, bq, bv],
    )
    kv_sibling = to_sibling(kv_h)
    p_h, *o_blocks = kernel_call(
        functools.partial(row_attend_kernel, heads, half, score_scale),
        "row_attend",
        (),
        [((heads, here, 2 * here), b16)] + [((heads, half, PAIR), b16)] * mps,
        [],
        8 * heads * here * here * PAIR,
        [q_h, kv_h, kv_sibling, mask_near],
    )
    o_from = [o_blocks[0]] + [shifted(o_blocks[k], -k) for k in range(1, mps)]

    weight_scratch = [pltpu.VMEM((mps, hs, width), b16)] * 5 + [bf_dma((20,))]
    square = tokens * width * width * 2
    row_heads, row_stream, col_normed, col_q, col_k, col_v, col_heads, col_stream, ffn_normed = (
        kernel_call(
            functools.partial(column_kernel, mps, heads),
            "column",
            (1, 2),
            [
                ((tokens, width), kind)
                for kind in (b16, f32, b16, b16, b16, b16, b16, f32, b16)
            ],
            weight_scratch,
            5 * square,
            [stream, own_attention, whole, row_bo, ln_col_gain, ln_col_bias, bq, bv]
            + [col_bo, ln_ffn_gain, ln_ffn_bias]
            + o_from,
        )
    )

    out_low, ffn_grad, col_low, grad_ffn, ffn_sums, grad_b1 = kernel_call(
        ffn_kernel,
        "ffn",
        (4, 5, 6),
        [
            ((tokens, width), b16),
            ((tokens, width), f32),
            ((tokens, width), b16),
            ((ranks, mps, dc, 2 * fs), b16),
            ((8, width), f32),
            ((mps, fs), f32),
        ],
        [
            pltpu.VMEM((mps, ranks, dc, fs), b16),
            pltpu.VMEM((mps, ranks, fc, width), b16),
            pltpu.VMEM((mps, ranks, dc, 2 * fs), b16),
            pltpu.VMEM((width, tokens), b16),
            pltpu.VMEM((width, tokens), b16),
            pltpu.VMEM((tokens, width), f32),
            pltpu.VMEM((tokens, width), f32),
            bf_dma((2 * mps,)),
            bf_dma((mps,)),
        ],
        12 * tokens * width * fs * mps,
        [rank_ref, ffn_normed, col_stream, grad_start, own_w1, own_w2, whole, b1, ffn_b2]
        + [ln_ffn_gain],
        (0,),
        out_places=(3,),
    )

    grad_q, grad_k, grad_v, row_grad, row_low, col_sums, *d_blocks = kernel_call(
        functools.partial(column_back_kernel, mps, heads),
        "column_back",
        (6, 7),
        [
            ((tokens, width), b16),
            ((tokens, width), b16),
            ((tokens, width), b16),
            ((tokens, width), f32),
            ((tokens, width), b16),
            ((8, width), f32),
        ]
        + [((heads, half, PAIR), b16)] * mps,
        weight_scratch,
        5 * square,
        [ffn_grad, col_low, col_q, col_k, col_v, row_stream, own_attention, whole]
        + [ln_col_gain],
    )
    d_from = [d_blocks[0]] + [shifted(d_blocks[k], -k) for k in range(1, mps)]
    def both(a, b, here):
        return a[here].astype(f32) + b[here].astype(f32)

    gq_h, gkv_h, gkv_theirs = kernel_call(
        functools.partial(row_attend_back_kernel, heads, half, mps, score_scale),
        "row_attend_back",
        (),
        [
            ((heads, here, PAIR), b16),
            ((2 * heads, here, PAIR), f32),
            ((2 * heads, here, PAIR), b16),
        ],
        [],
        16 * heads * here * here * PAIR,
        [q_h, kv_h, kv_sibling, p_h] + [d_from[-k % mps] for k in range(mps)],
    )
    gkv_sibling = to_sibling(gkv_theirs)
    lanes = -(-5 * hs // 128) * 128
    *att_keep, att_send0, att_send1 = kernel_call(
        weights_kernel,
        "weights",
        (),
        [((2, width // 2, lanes), b16)] * 4,
        [
            pltpu.VMEM((9, width, tokens), b16),
            pltpu.VMEM((2, 2, width, lanes), b16),
            bf_dma((8,)),
        ],
        5 * square,
        [rank_ref, col_normed, col_low, row_low, grad_q, grad_k, grad_v, col_heads, row_heads],
        (0,),
        [gkv_sibling],
        (0, 1, 2, 3),
    )
    row_keep, row_theirs, row_bias, *g_send = kernel_call(
        functools.partial(row_project_back_kernel, mps, half, heads),
        "row_project_back",
        (),
        [
            ((width // 2, row_width), b16),
            ((width // 2, row_width), b16),
            ((1, row_width), f32),
        ]
        + [((tokens + 16, width), b16)] * mps,
        [
            pltpu.VMEM((16, width), f32),
            pltpu.VMEM((mps * tokens, row_width), b16),
            pltpu.VMEM((width, row_width), f32),
        ],
        4 * mps * tokens * width * row_width,
        [rank_ref] + hidden + [row_w, ln_row_gain, ln_row_bias, gq_h, gkv_h, gkv_sibling]
        + [col_sums, ffn_sums, grad_b1],
        (0,),
        att_keep,
    )
    part = width // 4
    upper, lower = slice(0, part // 2), slice(part // 2, part)
    *att_theirs, row_keep = together(to_sibling(att_send0), to_sibling(att_send1), row_keep)
    hops = ((to_x, to_y), (to_y, to_x))

    def chip_sum(i, here):
        return att_keep[i][:, here].astype(f32) + att_theirs[i][:, here].astype(f32)

    got = together(
        *(shifted(g_send[k], -k) for k in range(1, mps)),
        *(hops[i][0](low(chip_sum(i, slice(part, None)))) for i in range(2)),
        to_sibling(row_theirs),
        lax.psum_scatter(grad_ffn, (DP, SEQ), scatter_dimension=0, tiled=True)[0],
    )
    first, row_peer, ffn_mine = got[mps - 1 : -2], got[-2], got[-1]
    ffn_total = lax.psum_scatter(ffn_mine, MP, scatter_dimension=0, tiled=True)[0].astype(f32)
    g_sum = sum(g.astype(f32) for g in (g_send[0], *got[: mps - 1]))
    gradient = row_grad + norm_pull(row_unit, row_scale, ln_row_gain, g_sum[:tokens])

    summed = jnp.concatenate(
        [g_sum[tokens : tokens + 12], jnp.pad(row_bias, ((0, 0), (0, width - row_width)))]
    )

    *second, their_sum, gradient = together(
        *(
            hops[i][1](low(chip_sum(i, lower) + first[i][:, lower].astype(f32)))
            for i in range(2)
        ),
        to_sibling(summed),
        gradient,
    )
    summed = summed + their_sum
    finals = [
        chip_sum(i, upper) + first[i][:, upper].astype(f32) + second[i].astype(f32)
        for i in range(2)
    ]
    shards = [finals[k // 2][k % 2] for k in range(mps)]

    def to_xy(values):
        return routed(values, lambda d, s, m: (d ^ 2, s ^ 1, m))

    quarter = part // 2
    row_sums = [both(row_keep, row_peer, slice(i * quarter, (i + 1) * quarter)) for i in range(4)]
    row_go = [low(v) for v in row_sums[1:]]
    *shards, row_go[0] = together(*shards, row_go[0])
    attention_total = shards[0]
    for k in range(1, mps):
        attention_total += shifted(low(shards[k]), -k).astype(f32)
    attention_total = attention_total[:, : 5 * hs].reshape(part // 2, 5, hs)
    out, grad_acts = kernel_call(
        home_kernel,
        "home",
        (),
        [((1, tokens, 1, width), f32)] * 2,
        [],
        0,
        [lax.axis_index(SEQ).reshape(1).astype(jnp.int32)]
        + list(send_from_work([out_low, low(gradient)])),
        (0,),
    )
    row_total = row_sums[0]
    for hop, values in zip((to_y, to_x, to_xy), row_go):
        row_total += hop(values).astype(f32)
    summed = summed + to_x(summed) + (to_y(summed) + to_xy(summed))
    device = rank * mps + z
    vectors = summed[:9].reshape(9, ranks * mps, -1)
    vectors = lax.dynamic_index_in_dim(vectors, device, axis=1, keepdims=False)

    def transposed(v):
        return v.T[None]

    return (
        out,
        grad_acts,
        vectors[0][None],
        vectors[1][None],
        row_total[:, :hs][None],
        row_total[:, hs : 2 * hs][None],
        row_total[:, 2 * hs : 3 * hs][None],
        summed[12:13, :hs],
        summed[12:13, 2 * hs : 3 * hs],
        transposed(attention_total[:, 4]),
        vectors[2][None],
        vectors[3][None],
        vectors[4][None],
        attention_total[:, 0][None],
        attention_total[:, 1][None],
        attention_total[:, 2][None],
        summed[9:10, :hs],
        summed[10:11, :hs],
        transposed(attention_total[:, 3]),
        vectors[5][None],
        vectors[6][None],
        vectors[7][None],
        ffn_total[:, :fs][None],
        summed[11:12],
        transposed(ffn_total[:, fs:]),
        vectors[8][None],
    )


def solution(mesh):
    placed = (
        P(DP, MP, SEQ, None),
        P(DP, MP, SEQ, None),
        P(DP, None),
        P(),
        P(),
        P(None, None, MP),
        P(None, None, MP),
        P(None, None, MP),
        P(None, MP),
        P(None, MP),
        P(None, MP, None),
        P(),
        P(),
        P(),
        P(None, None, MP),
        P(None, None, MP),
        P(None, None, MP),
        P(None, MP),
        P(None, MP),
        P(None, MP, None),
        P(),
        P(),
        P(),
        P(None, None, MP),
        P(None, MP),
        P(None, MP, None),
        P(),
    )
    in_pairs = tuple(mesh.shape[axis] for axis in AXES) == (4, 2, 4)
    return jax.shard_map(
        on_device_columns if in_pairs else on_device,
        mesh=mesh,
        in_specs=placed,
        out_specs=(
            P(DP, MP, SEQ, None),
            P(DP, MP, SEQ, None),
            P(None, (DP, SEQ, MP)),
            P(None, (DP, SEQ, MP)),
            P(None, (DP, SEQ), MP),
            P(None, (DP, SEQ), MP),
            P(None, (DP, SEQ), MP),
            P(None, MP),
            P(None, MP),
            P(None, MP, (DP, SEQ)),
            P(None, (DP, SEQ, MP)),
            P(None, (DP, SEQ, MP)),
            P(None, (DP, SEQ, MP)),
            P(None, (DP, SEQ), MP),
            P(None, (DP, SEQ), MP),
            P(None, (DP, SEQ), MP),
            P(None, MP),
            P(None, MP),
            P(None, MP, (DP, SEQ)),
            P(None, (DP, SEQ, MP)),
            P(None, (DP, SEQ, MP)),
            P(None, (DP, SEQ, MP)),
            P(None, (DP, SEQ), MP),
            P(None, MP),
            P(None, MP, (DP, SEQ)),
            P(None, (DP, SEQ, MP)),
        ),
        check_vma=False,
    )
```
